32 devices in a mesh: dom: 4 (over x, core), sub: 8 (over z, y).
Axes of the slice: x: 2, y: 2, z: 4, core: 2. Of those that a mesh axis runs over, the one named last changes fastest.
Arguments:
- feats: bfloat16 [65536, 256], P(('dom', 'sub')), may hold values from -6 to 6
- w_self: bfloat16 [256, 256], replicated, may hold values from -0.375 to 0.375
- w_neigh: bfloat16 [256, 256], replicated, may hold values from -0.375 to 0.375
- cotangent: bfloat16 [65536, 256], P(('dom', 'sub')), may hold values from -6 to 6
- hub_rows: int32 [1024], P(('dom', 'sub')), may hold values from 0 to 2047
- send_rows: int32 [16384], P(('dom', 'sub')), may hold values from 0 to 2047
- edge_src: int32 [2097152], P(('dom', 'sub')), may hold values from 0 to 3583
- edge_dst: int32 [2097152], P(('dom', 'sub')), may hold values from 0 to 2047
Outputs:
- layer_out: bfloat16 [65536, 256], P(('dom', 'sub'))
- grad_feats: bfloat16 [65536, 256], P(('dom', 'sub'))
- grad_self: float32 [256, 256], replicated
- grad_neigh: float32 [256, 256], replicated
The draws below stay inside these ranges and needn't reach their ends.
All inputs are finite; a program needn't handle non-finite values.
Results may differ from the reference program's by a relative error of at most 0.0051.
Values may be sent and summed in bfloat16 or wider, within the bound.
No kernel may reach another device: no remote copies, remote signals or barrier semaphores. Data moves between devices by JAX's collectives and lax.ppermute only.
A program may use at most 320 MiB of HBM per device.

```python
import jax
import jax.numpy as jnp
from jax import lax

F = 256
H = 256
V_DEV = 2048
E_DEV = 65536
HUB_DEV = 32
CAP = 16
VERTS = 65536
SLOTS = 3584
DEVICES = 32


def touch_ends(entries, own_key, smallest, top_value):
    dims = entries.shape
    spot = [jax.random.randint(jax.random.fold_in(own_key, axis), (), 0, dims[axis]) for axis in range(len(dims))]
    entries = entries.at[tuple(spot)].set(smallest)
    longest = dims.index(max(dims))
    spot[longest] = (spot[longest] + 1) % dims[longest]
    return entries.at[tuple(spot)].set(top_value)


def level_of(stream_key, dims, pieces, smallest, top_value):
    def one(position, blocks):
        heights = jax.random.uniform(jax.random.fold_in(jax.random.fold_in(stream_key, 6), position), (blocks,), jnp.float32, smallest / len(pieces), top_value / len(pieces))
        return jnp.repeat(jnp.exp(heights), dims[position] // blocks).reshape((-1,) + (1,) * (len(dims) - position - 1))

    loudness = one(*pieces[0])
    for cut in pieces[1:]:
        loudness = loudness * one(*cut)
    return loudness


def bell_draw(rng, dims, width, most, pieces=(), held_as=jnp.bfloat16):
    entries = jax.random.normal(rng, dims, jnp.float32) * width
    if len(pieces) > 0:
        entries = level_of(rng, dims, pieces, -0.22, 0.18) * entries
    return jnp.clip(entries, min=-most, max=most).astype(held_as)


def setup_inputs(seed: int = 0) -> dict:
    seeds = jax.random.split(jax.random.key(seed), 9)
    feats = bell_draw(seeds[0], (VERTS, F), 1.0, 6.0, ((0, 32),))
    w_self = bell_draw(seeds[1], (F, H), F ** -0.5, 0.375)
    w_neigh = bell_draw(seeds[2], (F, H), F ** -0.5, 0.375)
    cotangent = bell_draw(seeds[3], (VERTS, H), 1.0, 6.0, ((0, 32),))
    hub_rows = touch_ends(jax.random.randint(seeds[4], (HUB_DEV * DEVICES,), 0, V_DEV), jax.random.fold_in(seeds[4], 1), 0, V_DEV - 1).astype(jnp.int32)
    send_rows = touch_ends(jax.random.randint(seeds[5], (CAP * DEVICES * DEVICES,), 0, V_DEV), jax.random.fold_in(seeds[5], 1), 0, V_DEV - 1).astype(jnp.int32)
    edge_src = touch_ends(jax.random.randint(seeds[6], (E_DEV * DEVICES,), 0, SLOTS), jax.random.fold_in(seeds[6], 1), 0, SLOTS - 1).astype(jnp.int32)
    edge_dst = touch_ends(jax.random.randint(seeds[7], (E_DEV * DEVICES,), 0, V_DEV), jax.random.fold_in(seeds[7], 1), 0, V_DEV - 1).astype(jnp.int32)
    return {"feats": feats, "w_self": w_self, "w_neigh": w_neigh, "cotangent": cotangent, "hub_rows": hub_rows, "send_rows": send_rows, "edge_src": edge_src, "edge_dst": edge_dst}


def silu_parts(pre):
    sig = jax.nn.sigmoid(pre)
    return pre * sig, sig * (1.0 + pre * (1.0 - sig))


def reference(feats, w_self, w_neigh, cotangent, hub_rows, send_rows, edge_src, edge_dst):
    count = DEVICES
    blocks = feats.reshape(count, V_DEV, F)
    hub_table = hub_rows.reshape(count, HUB_DEV)
    hubs = jax.vmap(lambda f, r: f[r])(blocks, hub_table).reshape(count * HUB_DEV, F)
    send_table = send_rows.reshape(count, count * CAP)
    sent = jax.vmap(lambda f, r: f[r])(blocks, send_table).reshape(count, count, CAP, F)
    received = jnp.transpose(sent, (1, 0, 2, 3)).reshape(count, count * CAP, F)
    sources = edge_src.reshape(count, E_DEV)
    targets = edge_dst.reshape(count, E_DEV)

    def forward_one(item):
        own, recv, src, dst = item
        table = jnp.concatenate([own, hubs, recv], axis=0)
        degree = jax.ops.segment_sum(jnp.ones((E_DEV,), jnp.float32), dst, num_segments=V_DEV)
        inverse = 1.0 / jnp.maximum(degree, 1.0)
        total = jax.ops.segment_sum(table[src].astype(jnp.float32), dst, num_segments=V_DEV)
        return (total * inverse[:, None]).astype(jnp.bfloat16), inverse

    mean, inverse = lax.map(forward_one, (blocks, received, sources, targets))
    mean = mean.reshape(count * V_DEV, F)
    inverse = inverse.reshape(count * V_DEV)
    pre = jnp.dot(feats, w_self, preferred_element_type=jnp.float32) + jnp.dot(mean, w_neigh, preferred_element_type=jnp.float32)
    act, slope = silu_parts(pre)
    layer_out = act.astype(jnp.bfloat16)
    grad_pre = (cotangent.astype(jnp.float32) * slope).astype(jnp.bfloat16)
    grad_self = jnp.dot(feats.T, grad_pre, preferred_element_type=jnp.float32)
    grad_neigh = jnp.dot(mean.T, grad_pre, preferred_element_type=jnp.float32)
    dmsg = (jnp.dot(grad_pre, w_neigh.T, preferred_element_type=jnp.float32) * inverse[:, None]).astype(jnp.bfloat16)
    dmsg = dmsg.reshape(count, V_DEV, F)

    def backward_one(hub_sum, item):
        msg, src, dst = item
        slot = jax.ops.segment_sum(msg[dst].astype(jnp.float32), src, num_segments=SLOTS)
        local = slot[:V_DEV]
        hub_part = slot[V_DEV:V_DEV + count * HUB_DEV]
        halo_part = slot[V_DEV + count * HUB_DEV:]
        return hub_sum + hub_part, (local, halo_part)

    hub_sum, (local, halo_part) = lax.scan(backward_one, jnp.zeros((count * HUB_DEV, F), jnp.float32), (dmsg, sources, targets))
    returned = jnp.transpose(halo_part.reshape(count, count, CAP, F), (1, 0, 2, 3)).reshape(count, count * CAP, F)
    hub_back = hub_sum.reshape(count, HUB_DEV, F)

    def assemble(item):
        rows_h, back_h, rows_s, back_s = item
        return jax.ops.segment_sum(back_h, rows_h, num_segments=V_DEV) + jax.ops.segment_sum(back_s, rows_s, num_segments=V_DEV)

    extra = lax.map(assemble, (hub_table, hub_back, send_table, returned)).reshape(count * V_DEV, F)
    grad_feats = jnp.dot(grad_pre, w_self.T, preferred_element_type=jnp.float32) + local.reshape(count * V_DEV, F) + extra
    return layer_out, grad_feats.astype(jnp.bfloat16), grad_self, grad_neigh
```

```python
import functools
import math

import jax
import jax.numpy as jnp
from jax import lax
from jax.experimental import pallas as pl
from jax.experimental.pallas import tpu as pltpu
from jax.sharding import PartitionSpec as P

AXES = ("dom", "sub")
T = 256
LANES = 128


def one_hot_rows(index_row, base, rows):
    lane_index = lax.broadcasted_iota(jnp.int32, (rows, index_row.shape[1]), 0)
    return (lane_index == (index_row - base)).astype(jnp.float32).astype(jnp.bfloat16)


def outer_nt(a, b):
    return lax.dot_general(a, b, (((1,), (1,)), ((), ())), preferred_element_type=jnp.float32)


def outer_tn(a, b):
    return lax.dot_general(a, b, (((0,), (0,)), ((), ())), preferred_element_type=jnp.float32)


def mm(a, b):
    return jnp.dot(a, b, preferred_element_type=jnp.float32)


def layer_kernel(
    first_ref, last_ref, flag_ref,
    keys_ref, feats_ref, remote_ref, ws_ref, wn_ref, cot_ref,
    out_ref, base_ref, back_ref, gs_ref, gn_ref,
    adj_ref, slot_ref, deg_ref, tile_ref,
    *, own_tiles, all_tiles, window, unroll,
):
    block = pl.program_id(0)
    steps = pl.num_programs(0)
    key_rows = keys_ref.shape[0]

    def tile_part(tile, row, count):
        left = []
        right = []
        for q in range(count):
            keys = keys_ref[pl.ds(row + q, 1), :]
            left.append(one_hot_rows(keys >> 8, tile * T, T))
            right.append(one_hot_rows(keys & 255, 0, T))
        return outer_nt(jnp.concatenate(left, axis=1), jnp.concatenate(right, axis=1))

    deg_ref[...] = jnp.zeros_like(deg_ref)

    def build(j, carry):
        tile = block * all_tiles + j
        start = jnp.minimum(first_ref[tile], key_rows - window)
        counts = tile_part(tile, start, window)
        deg_ref[...] += counts[:, :LANES] + counts[:, LANES:]
        adj_ref[:, pl.ds(pl.multiple_of(j * T, T), T)] = counts.astype(jnp.bfloat16)
        return carry

    lax.fori_loop(0, all_tiles, build, 0, unroll=unroll)

    @pl.when(flag_ref[block] > 0)
    def _():
        def rest(j, carry):
            tile = block * all_tiles + j
            start = jnp.minimum(first_ref[tile], key_rows - window)
            stop = last_ref[tile]

            @pl.when(stop > start + window)
            def _():
                tile_ref[...] = tile_part(tile, start, window)

                def more(row, inner):
                    counts = tile_part(tile, row, 1)
                    deg_ref[...] += counts[:, :LANES] + counts[:, LANES:]
                    tile_ref[...] += counts
                    return inner

                lax.fori_loop(start + window, stop, more, 0)
                adj_ref[:, pl.ds(pl.multiple_of(j * T, T), T)] = tile_ref[...].astype(jnp.bfloat16)

            return carry

        lax.fori_loop(0, all_tiles, rest, 0)

    own = own_tiles * T
    total = mm(adj_ref[:, :own], feats_ref[...]) + mm(adj_ref[:, own:], remote_ref[...])
    degree = jnp.sum(deg_ref[...], axis=1, keepdims=True)
    inverse = 1.0 / jnp.maximum(degree, 1.0)
    mean = (total * inverse).astype(jnp.bfloat16)
    mine = feats_ref[pl.ds(pl.multiple_of(block * T, T), T), :]
    pre = mm(mine, ws_ref[...]) + mm(mean, wn_ref[...])
    sig = jax.nn.sigmoid(pre)
    out_ref[...] = (pre * sig).astype(jnp.bfloat16)
    slope = sig * (1.0 + pre * (1.0 - sig))
    grad_pre = (cot_ref[...].astype(jnp.float32) * slope).astype(jnp.bfloat16)

    part_self = outer_tn(mine, grad_pre)
    part_neigh = outer_tn(mean, grad_pre)

    @pl.when(block == 0)
    def _():
        gs_ref[...] = part_self
        gn_ref[...] = part_neigh
        slot_ref[...] = jnp.zeros_like(slot_ref)

    @pl.when(block > 0)
    def _():
        gs_ref[...] += part_self
        gn_ref[...] += part_neigh

    base_ref[pl.ds(pl.multiple_of(block * T, T), T), :] = outer_nt(grad_pre, ws_ref[...])
    dmsg = outer_nt(grad_pre, wn_ref[...]) * inverse
    dmsg_t = dmsg.T.astype(jnp.bfloat16)

    def spread(j, carry):
        cols = pl.ds(pl.multiple_of(j * T, T), T)
        slot_ref[:, cols] += mm(dmsg_t, adj_ref[:, cols])
        return carry

    lax.fori_loop(0, all_tiles, spread, 0, unroll=2)

    @pl.when(block == steps - 1)
    def _():
        def own_rows(j, carry):
            at = pl.ds(pl.multiple_of(j * T, T), T)
            base_ref[at, :] += slot_ref[:, at].T
            return carry

        lax.fori_loop(0, own_tiles, own_rows, 0)

        def far_rows(j, carry):
            at = pl.ds(pl.multiple_of(j * T, T), T)
            cols = pl.ds(pl.multiple_of(own + j * T, T), T)
            back_ref[at, :] = slot_ref[:, cols].T.astype(jnp.bfloat16)
            return carry

        lax.fori_loop(0, all_tiles - own_tiles, far_rows, 0)


def finish_kernel(index_ref, base_ref, back_ref, out_ref):
    block = pl.program_id(0)
    pick = one_hot_rows(index_ref[...], block * T, T)
    out_ref[...] = (base_ref[...] + mm(pick, back_ref[...])).astype(jnp.bfloat16)


def body(feats, w_self, w_neigh, cotangent, hub_rows, send_rows, edge_src, edge_dst):
    devices = lax.axis_size("dom") * lax.axis_size("sub")
    vcount, width = feats.shape
    edges = edge_src.shape[0]
    hub_dev = hub_rows.shape[0]
    cap = send_rows.shape[0] // devices
    pack = hub_dev + cap
    far = devices * pack
    slots = vcount + far
    own_tiles = vcount // T
    all_tiles = slots // T
    tiles = own_tiles * all_tiles
    key_rows = edges // LANES

    send_table = send_rows.reshape(devices, cap)
    hub_out = jnp.broadcast_to(feats[hub_rows][None], (devices, hub_dev, width))
    halo_out = feats[send_rows].reshape(devices, cap, width)
    outgoing = jnp.concatenate([hub_out, halo_out], axis=1)
    remote = lax.all_to_all(outgoing, AXES, split_axis=0, concat_axis=0, tiled=True)
    remote = remote.reshape(far, width)

    hub_at = edge_src - vcount
    halo_at = hub_at - devices * hub_dev
    hub_slot = vcount + (hub_at // hub_dev) * pack + hub_at % hub_dev
    halo_slot = vcount + (halo_at // cap) * pack + hub_dev + halo_at % cap
    slot = jnp.where(hub_at < 0, edge_src, jnp.where(halo_at < 0, hub_slot, halo_slot))
    tile_id = (edge_dst // T) * all_tiles + slot // T
    key = (tile_id * T + edge_dst % T) * T + slot % T
    keys = lax.sort(key, is_stable=False).reshape(key_rows, LANES)
    heads = keys[:, 0]
    limits = jnp.arange(tiles + 1, dtype=jnp.int32) * (T * T)
    below = jnp.sum((heads[None, :] < limits[:, None]).astype(jnp.int32), axis=1)
    first = jnp.maximum(below[:-1] - 1, 0)
    last = below[1:]
    average = edges / tiles
    window = min(key_rows, math.ceil((average + LANES + 2.0 * math.sqrt(average)) / LANES))
    over = (last > jnp.minimum(first, key_rows - window) + window).astype(jnp.int32)
    flags = jnp.max(over.reshape(own_tiles, all_tiles), axis=1)

    whole = lambda b, *_: (0, 0)
    by_block = lambda b, *_: (b, 0)
    f32 = jnp.float32
    bf16 = jnp.bfloat16
    layer_out, base, back, part_self, part_neigh = pl.pallas_call(
        functools.partial(
            layer_kernel, own_tiles=own_tiles, all_tiles=all_tiles, window=window, unroll=2
        ),
        name="layer",
        out_shape=(
            jax.ShapeDtypeStruct((vcount, width), bf16),
            jax.ShapeDtypeStruct((vcount, width), f32),
            jax.ShapeDtypeStruct((far, width), bf16),
            jax.ShapeDtypeStruct((width, width), f32),
            jax.ShapeDtypeStruct((width, width), f32),
        ),
        grid_spec=pltpu.PrefetchScalarGridSpec(
            num_scalar_prefetch=3,
            grid=(own_tiles,),
            in_specs=[
                pl.BlockSpec((key_rows, LANES), whole),
                pl.BlockSpec((vcount, width), whole),
                pl.BlockSpec((far, width), whole),
                pl.BlockSpec((width, width), whole),
                pl.BlockSpec((width, width), whole),
                pl.BlockSpec((T, width), by_block),
            ],
            out_specs=[
                pl.BlockSpec((T, width), by_block),
                pl.BlockSpec((vcount, width), whole),
                pl.BlockSpec((far, width), whole),
                pl.BlockSpec((width, width), whole),
                pl.BlockSpec((width, width), whole),
            ],
            scratch_shapes=[
                pltpu.VMEM((T, slots), bf16),
                pltpu.VMEM((width, slots), f32),
                pltpu.VMEM((T, LANES), f32),
                pltpu.VMEM((T, T), f32),
            ],
        ),
        compiler_params=pltpu.CompilerParams(
            dimension_semantics=("arbitrary",), vmem_limit_bytes=48 << 20
        ),
    )(first, last, flags, keys, feats, remote, w_self, w_neigh, cotangent)

    parts = jnp.concatenate([part_self, part_neigh], axis=0)
    share = parts.shape[0] // devices
    parts = parts.reshape(devices, share, width)
    parts = lax.all_to_all(parts, AXES, split_axis=0, concat_axis=0, tiled=True)
    mine = jnp.sum(parts, axis=0)
    grads = jnp.broadcast_to(mine[None], (devices, share, width))
    grads = lax.all_to_all(grads, AXES, split_axis=0, concat_axis=0, tiled=True)
    grads = grads.reshape(2 * width, width)

    returned = lax.all_to_all(
        back.reshape(devices, pack, width), AXES, split_axis=0, concat_axis=0, tiled=True
    ).reshape(far, width)
    index = jnp.concatenate(
        [jnp.broadcast_to(hub_rows[None], (devices, hub_dev)), send_table], axis=1
    ).reshape(1, far)
    grad_feats = pl.pallas_call(
        finish_kernel,
        name="finish",
        out_shape=jax.ShapeDtypeStruct((vcount, width), bf16),
        grid=(own_tiles,),
        in_specs=[
            pl.BlockSpec((1, far), lambda b: (0, 0)),
            pl.BlockSpec((T, width), lambda b: (b, 0)),
            pl.BlockSpec((far, width), lambda b: (0, 0)),
        ],
        out_specs=pl.BlockSpec((T, width), lambda b: (b, 0)),
        compiler_params=pltpu.CompilerParams(
            dimension_semantics=("arbitrary",), vmem_limit_bytes=32 << 20
        ),
    )(index, base, returned)
    return (layer_out, grad_feats, grads[:width], grads[width:])


def solution(mesh):
    return jax.shard_map(
        body,
        mesh=mesh,
        in_specs=(
            P(AXES, None),
            P(),
            P(),
            P(AXES, None),
            P(AXES),
            P(AXES),
            P(AXES),
            P(AXES),
        ),
        out_specs=(P(AXES, None), P(AXES, None), P(), P()),
        check_vma=False,
    )
```

```python
import functools
import math

import jax
import jax.numpy as jnp
from jax import lax
from jax.experimental import pallas as pl
from jax.experimental.pallas import tpu as pltpu
from jax.sharding import PartitionSpec as P

AXES = ("dom", "sub")
T = 256
LANES = 128
F8 = jnp.float8_e4m3fn


def outer_nt(a, b):
    return lax.dot_general(a, b, (((1,), (1,)), ((), ())), preferred_element_type=jnp.float32)


def outer_tn(a, b):
    return lax.dot_general(a, b, (((0,), (0,)), ((), ())), preferred_element_type=jnp.float32)


def mm(a, b):
    return jnp.dot(a, b, preferred_element_type=jnp.float32)


def counts_kernel(first_ref, last_ref, flag_ref, keys_ref, adj_ref, deg_ref, tile_ref,
                  *, all_tiles, window, unroll):
    block = pl.program_id(0)
    key_rows = keys_ref.shape[0]
    ids = (lax.broadcasted_iota(jnp.int32, (T, LANES), 0) - 128).astype(jnp.int8)
    none = jnp.zeros((T, LANES), F8)
    ones = jnp.ones((T, LANES), F8)

    def match(low):
        return ids == jnp.broadcast_to((low - 128).astype(jnp.int8), (T, LANES))

    def tile_part(tile, row, count):
        left = []
        right = []
        for q in range(count):
            keys = keys_ref[pl.ds(row + q, 1), :]
            inside = jnp.where((keys >> 16) == tile, 1.0, 0.0).astype(F8)
            left.append(
                jnp.where(match((keys >> 8) & 255), jnp.broadcast_to(inside, (T, LANES)), none)
            )
            right.append(jnp.where(match(keys & 255), ones, none))
        return outer_nt(jnp.concatenate(left, axis=1), jnp.concatenate(right, axis=1))

    deg_ref[...] = jnp.zeros_like(deg_ref)

    def build(j, carry):
        tile = block * all_tiles + j
        start = jnp.minimum(first_ref[tile], key_rows - window)
        counts = tile_part(tile, start, window)
        deg_ref[...] += counts[:, :LANES] + counts[:, LANES:]
        adj_ref[:, pl.ds(pl.multiple_of(j * T, T), T)] = counts.astype(jnp.bfloat16)
        return carry

    lax.fori_loop(0, all_tiles, build, 0, unroll=unroll)

    @pl.when(flag_ref[block] > 0)
    def _():
        def rest(j, carry):
            tile = block * all_tiles + j
            start = jnp.minimum(first_ref[tile], key_rows - window)
            stop = last_ref[tile]

            @pl.when(stop > start + window)
            def _():
                tile_ref[...] = tile_part(tile, start, window)

                def more(row, inner):
                    counts = tile_part(tile, row, 1)
                    deg_ref[...] += counts[:, :LANES] + counts[:, LANES:]
                    tile_ref[...] += counts
                    return inner

                lax.fori_loop(start + window, stop, more, 0)
                adj_ref[:, pl.ds(pl.multiple_of(j * T, T), T)] = tile_ref[...].astype(jnp.bfloat16)

            return carry

        lax.fori_loop(0, all_tiles, rest, 0)


def forward_kernel(adj_ref, deg_ref, feats_ref, remote_ref, ws_ref, wn_ref, cot_ref,
                   out_ref, g_ref, dmsg_ref, grads_ref):
    block = pl.program_id(0)
    rows, width = out_ref.shape
    own = feats_ref.shape[0]
    total = mm(adj_ref[:, :own], feats_ref[...]) + mm(adj_ref[:, own:], remote_ref[...])
    degree = jnp.sum(deg_ref[...], axis=1, keepdims=True)
    inverse = 1.0 / jnp.maximum(degree, 1.0)
    mean = (total * inverse).astype(jnp.bfloat16)
    mine = feats_ref[pl.ds(pl.multiple_of(block * rows, rows), rows), :]
    pre = mm(mine, ws_ref[...]) + mm(mean, wn_ref[...])
    sig = jax.nn.sigmoid(pre)
    out_ref[...] = (pre * sig).astype(jnp.bfloat16)
    slope = sig * (1.0 + pre * (1.0 - sig))
    g = (cot_ref[...].astype(jnp.float32) * slope).astype(jnp.bfloat16)
    g_ref[...] = g
    dmsg_ref[...] = (outer_nt(g, wn_ref[...]) * inverse).astype(jnp.bfloat16)

    @pl.when(block == 0)
    def _():
        grads_ref[...] = jnp.zeros_like(grads_ref)

    grads_ref[:width, :] += outer_tn(mine, g)
    grads_ref[width:, :] += outer_tn(mean, g)


def far_kernel(adj_ref, dmsg_ref, back_ref):
    back_ref[...] = outer_tn(adj_ref[...], dmsg_ref[...]).astype(jnp.bfloat16)


def own_kernel(adj_ref, dmsg_ref, g_ref, ws_ref, base_ref):
    base_ref[...] = outer_tn(adj_ref[...], dmsg_ref[...]) + outer_nt(g_ref[...], ws_ref[...])


def finish_kernel(index_ref, base_ref, back_ref, out_ref):
    block = pl.program_id(0)
    rows = out_ref.shape[0]
    far = index_ref.shape[1]
    spot = jnp.clip(index_ref[...] - block * rows, -1, rows).astype(jnp.int16)
    ids = lax.broadcasted_iota(jnp.int16, (rows, far), 0)
    pick = jnp.where(
        ids == jnp.broadcast_to(spot, (rows, far)),
        jnp.ones((rows, far), jnp.bfloat16),
        jnp.zeros((rows, far), jnp.bfloat16),
    )
    out_ref[...] = (base_ref[...] + mm(pick, back_ref[...])).astype(jnp.bfloat16)


def all_reduce(parts, gate):
    dom = lax.axis_size("dom")
    sub = lax.axis_size("sub")
    at = lax.axis_index("dom")
    steps = []
    stride = 1
    while stride < dom:
        half = parts.shape[0] // 2
        bit = (at // stride) % 2
        pairs = [(i, i ^ stride) for i in range(dom)]
        sent = lax.dynamic_slice_in_dim(parts, (1 - bit) * half, half, 0)
        kept = lax.dynamic_slice_in_dim(parts, bit * half, half, 0)
        came = lax.ppermute(sent, "dom", pairs)
        if stride == 1:
            came, gate = lax.optimization_barrier((came, gate))
        parts = kept + came
        steps.append((bit, pairs))
        stride *= 2
    stride = 1
    while stride < sub:
        parts = parts + lax.ppermute(parts, "sub", [(i, i ^ stride) for i in range(sub)])
        stride *= 2
    parts = parts.astype(jnp.bfloat16)
    for bit, pairs in reversed(steps):
        other = lax.ppermute(parts, "dom", pairs)
        low = jnp.where(bit == 0, parts, other)
        high = jnp.where(bit == 0, other, parts)
        parts = jnp.concatenate([low, high], axis=0)
    return parts.astype(jnp.float32), gate


def call(kernel, grid, in_specs, out_specs, out_shape, name, vmem):
    return pl.pallas_call(
        kernel,
        name=name,
        grid=grid,
        in_specs=in_specs,
        out_specs=out_specs,
        out_shape=out_shape,
        compiler_params=pltpu.CompilerParams(
            dimension_semantics=("arbitrary",), vmem_limit_bytes=vmem
        ),
    )


def body(feats, w_self, w_neigh, cotangent, hub_rows, send_rows, edge_src, edge_dst):
    devices = lax.axis_size("dom") * lax.axis_size("sub")
    vcount, width = feats.shape
    edges = edge_src.shape[0]
    hub_dev = hub_rows.shape[0]
    cap = send_rows.shape[0] // devices
    pack = hub_dev + cap
    far = devices * pack
    slots = vcount + far
    own_tiles = vcount // T
    all_tiles = slots // T
    tiles = own_tiles * all_tiles
    key_rows = edges // LANES
    f32 = jnp.float32
    bf16 = jnp.bfloat16

    send_table = send_rows.reshape(devices, cap)
    hub_out = jnp.broadcast_to(feats[hub_rows][None], (devices, hub_dev, width))
    halo_out = feats[send_rows].reshape(devices, cap, width)
    outgoing = jnp.concatenate([hub_out, halo_out], axis=1)
    remote = lax.all_to_all(outgoing, AXES, split_axis=0, concat_axis=0, tiled=True)
    remote = remote.reshape(far, width)

    hub_at = edge_src - vcount
    halo_at = hub_at - devices * hub_dev
    hub_slot = vcount + (hub_at // hub_dev) * pack + hub_at % hub_dev
    halo_slot = vcount + (halo_at // cap) * pack + hub_dev + halo_at % cap
    slot = jnp.where(hub_at < 0, edge_src, jnp.where(halo_at < 0, hub_slot, halo_slot))
    tile_id = (edge_dst // T) * all_tiles + slot // T
    key = (tile_id * T + edge_dst % T) * T + slot % T
    keys = lax.sort(key, is_stable=False).reshape(key_rows, LANES)
    heads = keys[:, 0]
    limits = jnp.arange(tiles + 1, dtype=jnp.int32) * (T * T)
    below = jnp.sum((heads[None, :] < limits[:, None]).astype(jnp.int32), axis=1)
    first = jnp.maximum(below[:-1] - 1, 0)
    last = below[1:]
    average = edges / tiles
    window = min(key_rows, math.ceil((average + LANES + 2.0 * math.sqrt(average)) / LANES))
    over = (last > jnp.minimum(first, key_rows - window) + window).astype(jnp.int32)
    flags = jnp.max(over.reshape(own_tiles, all_tiles), axis=1)
    unroll = max(u for u in range(1, 17) if all_tiles % u == 0)

    adj, deg = pl.pallas_call(
        functools.partial(counts_kernel, all_tiles=all_tiles, window=window, unroll=unroll),
        name="counts",
        out_shape=(
            pltpu.HBM((vcount, slots), bf16),
            pltpu.HBM((vcount, LANES), f32),
        ),
        grid_spec=pltpu.PrefetchScalarGridSpec(
            num_scalar_prefetch=3,
            grid=(own_tiles,),
            in_specs=[pl.BlockSpec((key_rows, LANES), lambda b, *_: (0, 0))],
            out_specs=[
                pl.BlockSpec((T, slots), lambda b, *_: (b, 0)),
                pl.BlockSpec((T, LANES), lambda b, *_: (b, 0)),
            ],
            scratch_shapes=[pltpu.VMEM((T, T), f32)],
        ),
        compiler_params=pltpu.CompilerParams(
            dimension_semantics=("arbitrary",), vmem_limit_bytes=(8 << 20) + 6 * T * slots
        ),
    )(first, last, flags, keys)

    adj = pltpu.with_memory_space_constraint(adj, pltpu.HBM)
    deg = pltpu.with_memory_space_constraint(deg, pltpu.HBM)
    whole = lambda b: (0, 0)
    by_row = lambda b: (b, 0)
    rows = min(2 * T, vcount)
    layer_out, g, dmsg, parts = call(
        forward_kernel,
        (vcount // rows,),
        [
            pl.BlockSpec((rows, slots), by_row),
            pl.BlockSpec((rows, LANES), by_row),
            pl.BlockSpec((vcount, width), whole),
            pl.BlockSpec((far, width), whole),
            pl.BlockSpec((width, width), whole),
            pl.BlockSpec((width, width), whole),
            pl.BlockSpec((rows, width), by_row),
        ],
        [
            pl.BlockSpec((rows, width), by_row),
            pl.BlockSpec((rows, width), by_row),
            pl.BlockSpec((rows, width), by_row),
            pl.BlockSpec((2 * width, width), whole),
        ],
        (
            pltpu.HBM((vcount, width), bf16),
            pltpu.HBM((vcount, width), bf16),
            pltpu.HBM((vcount, width), bf16),
            jax.ShapeDtypeStruct((2 * width, width), f32),
        ),
        "forward",
        (8 << 20) + 4 * rows * slots + 4 * slots * width,
    )(adj, deg, feats, remote, w_self, w_neigh, cotangent)

    g = pltpu.with_memory_space_constraint(g, pltpu.HBM)
    dmsg = pltpu.with_memory_space_constraint(dmsg, pltpu.HBM)
    cols = 2 * T
    skip = vcount // cols
    back = call(
        far_kernel,
        (far // cols,),
        [
            pl.BlockSpec((vcount, cols), lambda j: (0, j + skip)),
            pl.BlockSpec((vcount, width), whole),
        ],
        pl.BlockSpec((cols, width), by_row),
        jax.ShapeDtypeStruct((far, width), bf16),
        "far",
        16 << 20,
    )(adj, dmsg)
    grads, back = all_reduce(parts, back)
    returned = lax.all_to_all(
        back.reshape(devices, pack, width), AXES, split_axis=0, concat_axis=0, tiled=True
    ).reshape(far, width)
    base = call(
        own_kernel,
        (vcount // cols,),
        [
            pl.BlockSpec((vcount, cols), lambda j: (0, j)),
            pl.BlockSpec((vcount, width), whole),
            pl.BlockSpec((cols, width), by_row),
            pl.BlockSpec((width, width), whole),
        ],
        pl.BlockSpec((cols, width), by_row),
        jax.ShapeDtypeStruct((vcount, width), f32),
        "own",
        16 << 20,
    )(adj, dmsg, g, w_self)

    index = jnp.concatenate(
        [jnp.broadcast_to(hub_rows[None], (devices, hub_dev)), send_table], axis=1
    ).reshape(1, far)
    grad_feats = call(
        finish_kernel,
        (own_tiles,),
        [
            pl.BlockSpec((1, far), whole),
            pl.BlockSpec((T, width), by_row),
            pl.BlockSpec((far, width), whole),
        ],
        pl.BlockSpec((T, width), by_row),
        jax.ShapeDtypeStruct((vcount, width), bf16),
        "finish",
        (8 << 20) + 8 * far * width,
    )(index, base, returned)
    return (layer_out, grad_feats, grads[:width], grads[width:])


def solution(mesh):
    return jax.shard_map(
        body,
        mesh=mesh,
        in_specs=(
            P(AXES, None),
            P(),
            P(),
            P(AXES, None),
            P(AXES),
            P(AXES),
            P(AXES),
            P(AXES),
        ),
        out_specs=(P(AXES, None), P(AXES, None), P(), P()),
        check_vma=False,
    )
```

```python
import functools
import math

import jax
import jax.numpy as jnp
from jax import lax
from jax.experimental import pallas as pl
from jax.experimental.pallas import tpu as pltpu
from jax.sharding import PartitionSpec as P

AXES = ("dom", "sub")
T = 256
LANES = 128
F8 = jnp.float8_e4m3fn


def outer_nt(a, b):
    return lax.dot_general(a, b, (((1,), (1,)), ((), ())), preferred_element_type=jnp.float32)


def outer_tn(a, b):
    return lax.dot_general(a, b, (((0,), (0,)), ((), ())), preferred_element_type=jnp.float32)


def mm(a, b):
    return jnp.dot(a, b, preferred_element_type=jnp.float32)


def counts_kernel(first_ref, last_ref, flag_ref, keys_ref, adj_ref, deg_ref, tile_ref,
                  *, all_tiles, window, unroll):
    block = pl.program_id(0)
    key_rows = keys_ref.shape[0]
    ids = (lax.broadcasted_iota(jnp.int32, (T, LANES), 0) - 128).astype(jnp.int8)
    none = jnp.zeros((T, LANES), F8)
    ones = jnp.ones((T, LANES), F8)

    def match(low):
        return ids == jnp.broadcast_to((low - 128).astype(jnp.int8), (T, LANES))

    def tile_part(tile, row, count):
        left = []
        right = []
        for q in range(count):
            keys = keys_ref[pl.ds(row + q, 1), :]
            inside = jnp.where((keys >> 16) == tile, 1.0, 0.0).astype(F8)
            left.append(
                jnp.where(match((keys >> 8) & 255), jnp.broadcast_to(inside, (T, LANES)), none)
            )
            right.append(jnp.where(match(keys & 255), ones, none))
        return outer_nt(jnp.concatenate(left, axis=1), jnp.concatenate(right, axis=1))

    deg_ref[...] = jnp.zeros_like(deg_ref)

    def build(j, carry):
        tile = block * all_tiles + j
        start = jnp.minimum(first_ref[tile], key_rows - window)
        counts = tile_part(tile, start, window)
        deg_ref[...] += counts[:, :LANES] + counts[:, LANES:]
        adj_ref[:, pl.ds(pl.multiple_of(j * T, T), T)] = counts.astype(jnp.bfloat16)
        return carry

    lax.fori_loop(0, all_tiles, build, 0, unroll=unroll)

    @pl.when(flag_ref[block] > 0)
    def _():
        def rest(j, carry):
            tile = block * all_tiles + j
            start = jnp.minimum(first_ref[tile], key_rows - window)
            stop = last_ref[tile]

            @pl.when(stop > start + window)
            def _():
                tile_ref[...] = tile_part(tile, start, window)

                def more(row, inner):
                    counts = tile_part(tile, row, 1)
                    deg_ref[...] += counts[:, :LANES] + counts[:, LANES:]
                    tile_ref[...] += counts
                    return inner

                lax.fori_loop(start + window, stop, more, 0)
                adj_ref[:, pl.ds(pl.multiple_of(j * T, T), T)] = tile_ref[...].astype(jnp.bfloat16)

            return carry

        lax.fori_loop(0, all_tiles, rest, 0)


def forward_kernel(core_ref, adj_ref, deg_ref, feats_ref, remote_ref, ws_ref, wn_ref, cot_ref,
                   out_ref, g_ref, dmsg_ref, grads_ref, table_ref, *, chunk):
    block = pl.program_id(0)
    pairs = remote_ref.shape[0] // chunk // 2

    @pl.when(block == 0)
    def _():
        for half in range(2):
            for pair in range(pairs):
                start = (2 * pair + (core_ref[0] ^ half)) * chunk
                table_ref[pl.ds((half * pairs + pair) * chunk, chunk), :] = remote_ref[
                    pl.ds(pl.multiple_of(start, 16), chunk), :
                ]

    rows, width = out_ref.shape
    own = feats_ref.shape[0]
    total = mm(adj_ref[:, :own], feats_ref[...]) + mm(adj_ref[:, own:], table_ref[...])
    degree = jnp.sum(deg_ref[...], axis=1, keepdims=True)
    inverse = 1.0 / jnp.maximum(degree, 1.0)
    mean = (total * inverse).astype(jnp.bfloat16)
    mine = feats_ref[pl.ds(pl.multiple_of(block * rows, rows), rows), :]
    pre = mm(mine, ws_ref[...]) + mm(mean, wn_ref[...])
    sig = jax.nn.sigmoid(pre)
    out_ref[...] = (pre * sig).astype(jnp.bfloat16)
    slope = sig * (1.0 + pre * (1.0 - sig))
    g = (cot_ref[...].astype(jnp.float32) * slope).astype(jnp.bfloat16)
    g_ref[...] = g
    dmsg_ref[...] = (outer_nt(g, wn_ref[...]) * inverse).astype(jnp.bfloat16)

    @pl.when(block == 0)
    def _():
        grads_ref[...] = jnp.zeros_like(grads_ref)

    grads_ref[:width, :] += outer_tn(mine, g)
    grads_ref[width:, :] += outer_tn(mean, g)


def far_kernel(adj_ref, dmsg_ref, *refs):
    back_ref = refs[-1]
    back_ref[...] = outer_tn(adj_ref[...], dmsg_ref[...]).astype(jnp.bfloat16)


def own_kernel(adj_ref, dmsg_ref, g_ref, ws_ref, *refs):
    base_ref = refs[-1]
    base_ref[...] = outer_tn(adj_ref[...], dmsg_ref[...]) + outer_nt(g_ref[...], ws_ref[...])


def finish_kernel(index_ref, base_ref, back_ref, out_ref):
    block = pl.program_id(0)
    rows = out_ref.shape[0]
    far = index_ref.shape[1]
    spot = jnp.clip(index_ref[...] - block * rows, -1, rows).astype(jnp.int16)
    ids = lax.broadcasted_iota(jnp.int16, (rows, far), 0)
    pick = jnp.where(
        ids == jnp.broadcast_to(spot, (rows, far)),
        jnp.ones((rows, far), jnp.bfloat16),
        jnp.zeros((rows, far), jnp.bfloat16),
    )
    out_ref[...] = (base_ref[...] + mm(pick, back_ref[...])).astype(jnp.bfloat16)


def gather_kernel(hub_ref, send_ref, feats_ref, out_ref, wide_ref, hubs_ref, sends_ref):
    hub_dev = hubs_ref.shape[0]
    count = sends_ref.shape[0]
    devices = (out_ref.shape[0] - count) // hub_dev
    cap = count // devices
    pack = hub_dev + cap
    wide_ref[...] = feats_ref[...].astype(jnp.float32)

    def hub(i, carry):
        hubs_ref[pl.ds(i, 1), :] = wide_ref[pl.ds(hub_ref[i], 1), :]
        return carry

    def send(i, carry):
        sends_ref[pl.ds(i, 1), :] = wide_ref[pl.ds(send_ref[i], 1), :]
        return carry

    lax.fori_loop(0, hub_dev, hub, 0, unroll=8)
    lax.fori_loop(0, count, send, 0, unroll=16)
    hubs = hubs_ref[...].astype(jnp.bfloat16)

    def place(p, carry):
        out_ref[pl.ds(pl.multiple_of(p * pack, 16), hub_dev), :] = hubs
        halo = sends_ref[pl.ds(pl.multiple_of(p * cap, 16), cap), :].astype(jnp.bfloat16)
        out_ref[pl.ds(pl.multiple_of(p * pack + hub_dev, 16), cap), :] = halo
        return carry

    lax.fori_loop(0, devices, place, 0, unroll=4)


def tie(*arrays):
    return lax.optimization_barrier(arrays)


def call(kernel, grid, in_specs, out_specs, out_shape, name, vmem, aliases=None):
    return pl.pallas_call(
        kernel,
        name=name,
        input_output_aliases=aliases or {},
        grid=grid,
        in_specs=in_specs,
        out_specs=out_specs,
        out_shape=out_shape,
        compiler_params=pltpu.CompilerParams(
            dimension_semantics=("arbitrary",), vmem_limit_bytes=vmem
        ),
    )


def body(feats, w_self, w_neigh, cotangent, hub_rows, send_rows, edge_src, edge_dst):
    devices = lax.axis_size("dom") * lax.axis_size("sub")
    vcount, width = feats.shape
    edges = edge_src.shape[0]
    hub_dev = hub_rows.shape[0]
    cap = send_rows.shape[0] // devices
    pack = hub_dev + cap
    far = devices * pack
    slots = vcount + far
    own_tiles = vcount // T
    all_tiles = slots // T
    tiles = own_tiles * all_tiles
    key_rows = edges // LANES
    f32 = jnp.float32
    bf16 = jnp.bfloat16

    send_table = send_rows.reshape(devices, cap)
    outgoing = pl.pallas_call(
        gather_kernel,
        name="gather",
        out_shape=jax.ShapeDtypeStruct((far, width), bf16),
        grid_spec=pltpu.PrefetchScalarGridSpec(
            num_scalar_prefetch=2,
            grid=(1,),
            in_specs=[pl.BlockSpec((vcount, width), lambda b, *_: (0, 0))],
            out_specs=pl.BlockSpec((far, width), lambda b, *_: (0, 0)),
            scratch_shapes=[
                pltpu.VMEM((vcount, width), f32),
                pltpu.VMEM((hub_dev, width), f32),
                pltpu.VMEM((devices * cap, width), f32),
            ],
        ),
        compiler_params=pltpu.CompilerParams(
            dimension_semantics=("arbitrary",),
            vmem_limit_bytes=(4 << 20) + width * (8 * vcount + 8 * far),
        ),
    )(
        hub_rows,
        send_rows,
        pltpu.with_memory_space_constraint(feats, pltpu.HBM),
    ).reshape(devices, pack, width)
    remote = lax.all_to_all(outgoing, AXES, split_axis=0, concat_axis=0, tiled=True)
    remote = remote.reshape(far, width)

    hub_at = edge_src - vcount
    halo_at = hub_at - devices * hub_dev
    dom = lax.axis_size("dom")
    sub = lax.axis_size("sub")
    core = lax.axis_index("dom") % 2

    def place(device):
        d = lax.div(device, sub)
        return (((d ^ core) & 1) * (dom // 2) + (d >> 1)) * sub + lax.rem(device, sub)

    hub_slot = vcount + place(lax.div(hub_at, hub_dev)) * pack + lax.rem(hub_at, hub_dev)
    halo_slot = vcount + place(lax.div(halo_at, cap)) * pack + hub_dev + lax.rem(halo_at, cap)
    slot = jnp.where(hub_at < 0, edge_src, jnp.where(halo_at < 0, hub_slot, halo_slot))
    tile_id = (edge_dst >> 8) * all_tiles + (slot >> 8)
    key = (tile_id << 16) | ((edge_dst & 255) << 8) | (slot & 255)
    keys = lax.sort(key, is_stable=False).reshape(key_rows, LANES)
    heads = keys[:, 0]
    limits = jnp.arange(tiles + 1, dtype=jnp.int32) * (T * T)
    below = jnp.sum((heads[None, :] < limits[:, None]).astype(jnp.int32), axis=1)
    first = jnp.maximum(below[:-1] - 1, 0)
    last = below[1:]
    average = edges / tiles
    window = min(key_rows, math.ceil((average + LANES + 2.0 * math.sqrt(average)) / LANES))
    over = (last > jnp.minimum(first, key_rows - window) + window).astype(jnp.int32)
    flags = jnp.max(over.reshape(own_tiles, all_tiles), axis=1)
    unroll = max(u for u in range(1, 17) if all_tiles % u == 0)

    adj, deg = pl.pallas_call(
        functools.partial(counts_kernel, all_tiles=all_tiles, window=window, unroll=unroll),
        name="counts",
        out_shape=(
            pltpu.HBM((vcount, slots), bf16),
            pltpu.HBM((vcount, LANES), f32),
        ),
        grid_spec=pltpu.PrefetchScalarGridSpec(
            num_scalar_prefetch=3,
            grid=(own_tiles,),
            in_specs=[pl.BlockSpec((key_rows, LANES), lambda b, *_: (0, 0))],
            out_specs=[
                pl.BlockSpec((T, slots), lambda b, *_: (b, 0)),
                pl.BlockSpec((T, LANES), lambda b, *_: (b, 0)),
            ],
            scratch_shapes=[pltpu.VMEM((T, T), f32)],
        ),
        compiler_params=pltpu.CompilerParams(
            dimension_semantics=("arbitrary",), vmem_limit_bytes=(8 << 20) + 6 * T * slots
        ),
    )(first, last, flags, keys)

    adj = pltpu.with_memory_space_constraint(adj, pltpu.HBM)
    deg = pltpu.with_memory_space_constraint(deg, pltpu.HBM)
    whole = lambda b, *_: (0, 0)
    by_row = lambda b, *_: (b, 0)
    rows = min(2 * T, vcount)
    layer_out, g, dmsg, parts = pl.pallas_call(
        functools.partial(forward_kernel, chunk=sub * pack),
        name="forward",
        grid_spec=pltpu.PrefetchScalarGridSpec(
            num_scalar_prefetch=1,
            grid=(vcount // rows,),
            in_specs=[
                pl.BlockSpec((rows, slots), by_row),
                pl.BlockSpec((rows, LANES), by_row),
                pl.BlockSpec((vcount, width), whole),
                pl.BlockSpec((far, width), whole),
                pl.BlockSpec((width, width), whole),
                pl.BlockSpec((width, width), whole),
                pl.BlockSpec((rows, width), by_row),
            ],
            out_specs=[
                pl.BlockSpec((rows, width), by_row),
                pl.BlockSpec((rows, width), by_row),
                pl.BlockSpec((rows, width), by_row),
                pl.BlockSpec((2 * width, width), whole),
            ],
            scratch_shapes=[pltpu.VMEM((far, width), bf16)],
        ),
        out_shape=(
            pltpu.HBM((vcount, width), bf16),
            pltpu.HBM((vcount, width), bf16),
            pltpu.HBM((vcount, width), bf16),
            jax.ShapeDtypeStruct((2 * width, width), f32),
        ),
        compiler_params=pltpu.CompilerParams(
            dimension_semantics=("arbitrary",),
            vmem_limit_bytes=(8 << 20) + 4 * rows * slots + 6 * slots * width,
        ),
    )(
        jnp.reshape(core, (1,)).astype(jnp.int32),
        adj,
        deg,
        feats,
        remote,
        w_self,
        w_neigh,
        pltpu.with_memory_space_constraint(cotangent, pltpu.HBM),
    )

    g = pltpu.with_memory_space_constraint(g, pltpu.HBM)
    dmsg = pltpu.with_memory_space_constraint(dmsg, pltpu.HBM)
    half = devices // 2
    twin = [(i, i ^ 1) for i in range(dom)]
    groups = [
        [d * sub + i for d in range(c, dom, 2) for i in range(sub)] for c in range(2)
    ]

    def exchange(x):
        return lax.all_to_all(
            x, AXES, split_axis=0, concat_axis=0, axis_index_groups=groups, tiled=True
        )

    def far_part(start, dmsg):
        return call(
            far_kernel,
            (far // 2 // T,),
            [
                pl.BlockSpec((vcount, T), lambda j: (0, j + start // T)),
                pl.BlockSpec((vcount, width), whole),
            ],
            pl.BlockSpec((T, width), by_row),
            jax.ShapeDtypeStruct((far // 2, width), bf16),
            "far",
            16 << 20,
        )(adj, dmsg)

    sent = lax.dynamic_slice_in_dim(parts, (1 - core) * width, width, 0)
    kept = lax.dynamic_slice_in_dim(parts, core * width, width, 0)
    came = lax.ppermute(sent, "dom", twin)
    given = far_part(vcount + far // 2, dmsg)
    got = lax.ppermute(given, "dom", twin)
    dmsg, given = tie(dmsg, given)
    kept_slots = far_part(vcount, dmsg)
    came, kept_slots = tie(came, kept_slots)
    share = width // half
    piece = (kept + came).astype(bf16).reshape(half, share, width)
    kept_slots = kept_slots.reshape(half, pack, width)
    got = got.reshape(half, pack, width)
    hub_sum = kept_slots[:, :hub_dev].astype(f32) + got[:, :hub_dev].astype(f32)
    payload = jnp.concatenate(
        [hub_sum.astype(bf16), kept_slots[:, hub_dev:], got[:, hub_dev:], piece], axis=1
    )
    bundle = payload.shape[1]
    returned = exchange(payload)
    cols = 2 * T
    base = call(
        own_kernel,
        (vcount // cols,),
        [
            pl.BlockSpec((vcount, cols), lambda j: (0, j)),
            pl.BlockSpec((vcount, width), whole),
            pl.BlockSpec((cols, width), by_row),
            pl.BlockSpec((width, width), whole),
        ],
        pl.BlockSpec((cols, width), by_row),
        jax.ShapeDtypeStruct((vcount, width), f32),
        "own",
        16 << 20,
    )(adj, dmsg, g, w_self)

    mine = jnp.sum(returned[:, bundle - share :].astype(f32), axis=0).astype(bf16)
    mine, base = tie(mine, base)
    mine = exchange(jnp.broadcast_to(mine[None], (half, share, width))).reshape(width, width)
    table = send_rows.reshape(dom // 2, 2, sub, cap)
    near = lax.dynamic_index_in_dim(table, core, 1, keepdims=False).reshape(half, cap)
    away = lax.dynamic_index_in_dim(table, 1 - core, 1, keepdims=False).reshape(half, cap)
    index = jnp.concatenate(
        [
            jnp.broadcast_to(hub_rows[None], (half, hub_dev)),
            near,
            away,
            jnp.full((half, share), -1, jnp.int32),
        ],
        axis=1,
    ).reshape(1, half * bundle)
    grad_feats = call(
        finish_kernel,
        (vcount // rows,),
        [
            pl.BlockSpec((1, half * bundle), whole),
            pl.BlockSpec((rows, width), by_row),
            pl.BlockSpec((half * bundle, width), whole),
        ],
        pl.BlockSpec((rows, width), by_row),
        jax.ShapeDtypeStruct((vcount, width), bf16),
        "finish",
        (8 << 20) + 8 * far * width,
    )(index, base, returned.reshape(half * bundle, width))
    mine, grad_feats = tie(mine, grad_feats)
    other = lax.ppermute(mine, "dom", twin)
    grad_self = jnp.where(core == 0, mine, other).astype(f32)
    grad_neigh = jnp.where(core == 0, other, mine).astype(f32)
    return (layer_out, grad_feats, grad_self, grad_neigh)


def solution(mesh):
    return jax.shard_map(
        body,
        mesh=mesh,
        in_specs=(
            P(AXES, None),
            P(),
            P(),
            P(AXES, None),
            P(AXES),
            P(AXES),
            P(AXES),
            P(AXES),
        ),
        out_specs=(P(AXES, None), P(AXES, None), P(), P()),
        check_vma=False,
    )
```

```python
import functools
import math

import jax
import jax.numpy as jnp
from jax import lax
from jax.experimental import pallas as pl
from jax.experimental.pallas import tpu as pltpu
from jax.sharding import PartitionSpec as P

AXES = ("dom", "sub")
T = 256
LANES = 128
PACKED = 16
F8 = jnp.float8_e4m3fn


def outer_nt(a, b):
    return lax.dot_general(a, b, (((1,), (1,)), ((), ())), preferred_element_type=jnp.float32)


def outer_tn(a, b):
    return lax.dot_general(a, b, (((0,), (0,)), ((), ())), preferred_element_type=jnp.float32)


def mm(a, b):
    return jnp.dot(a, b, preferred_element_type=jnp.float32)


def counts_kernel(first_ref, last_ref, flag_ref, keys_ref, near_ref, far_ref, deg_ref, tile_ref,
                  *, own_tiles, all_tiles, window):
    block = pl.program_id(0)
    key_rows = keys_ref.shape[0]
    ids = (lax.broadcasted_iota(jnp.int32, (T, LANES), 0) - 128).astype(jnp.int8)
    none = jnp.zeros((T, LANES), F8)
    ones = jnp.ones((T, LANES), F8)

    def match(low):
        return ids == jnp.broadcast_to((low - 128).astype(jnp.int8), (T, LANES))

    def tile_part(tile, row, count):
        left = []
        right = []
        for q in range(count):
            keys = keys_ref[pl.ds(row + q, 1), :]
            inside = jnp.where((keys >> 16) == tile, 1.0, 0.0).astype(F8)
            left.append(
                jnp.where(match((keys >> 8) & 255), jnp.broadcast_to(inside, (T, LANES)), none)
            )
            right.append(jnp.where(match(keys & 255), ones, none))
        return outer_nt(jnp.concatenate(left, axis=1), jnp.concatenate(right, axis=1))

    deg_ref[...] = jnp.zeros_like(deg_ref)

    ranges = [(near_ref, 0, own_tiles), (far_ref, own_tiles, all_tiles - own_tiles)]

    for ref, shift, number in ranges:

        def build(j, carry, ref=ref, shift=shift):
            tile = block * all_tiles + shift + j
            start = jnp.minimum(first_ref[tile], key_rows - window)
            counts = tile_part(tile, start, window)
            deg_ref[...] += counts[:, :LANES] + counts[:, LANES:]
            ref[:, pl.ds(pl.multiple_of(j * T, T), T)] = counts.astype(jnp.bfloat16)
            return carry

        unroll = max(u for u in range(1, 13) if number % u == 0)
        lax.fori_loop(0, number, build, 0, unroll=unroll)

    @pl.when(flag_ref[block] > 0)
    def _():
        for ref, shift, number in ranges:

            def rest(j, carry, ref=ref, shift=shift):
                tile = block * all_tiles + shift + j
                start = jnp.minimum(first_ref[tile], key_rows - window)
                stop = last_ref[tile]

                @pl.when(stop > start + window)
                def _():
                    tile_ref[...] = tile_part(tile, start, window)

                    def more(row, inner):
                        counts = tile_part(tile, row, 1)
                        deg_ref[...] += counts[:, :LANES] + counts[:, LANES:]
                        tile_ref[...] += counts
                        return inner

                    lax.fori_loop(start + window, stop, more, 0)
                    cols = pl.ds(pl.multiple_of(j * T, T), T)
                    ref[:, cols] = tile_ref[...].astype(jnp.bfloat16)

                return carry

            lax.fori_loop(0, number, rest, 0)


def forward_kernel(core_ref, near_ref, far_ref, deg_ref, feats_ref, remote_ref, ws_ref, wn_ref, cot_ref,
                   out_ref, g_ref, dmsg_ref, grads_ref, table_ref, *, chunk):
    block = pl.program_id(0)
    pairs = remote_ref.shape[0] // chunk // 2

    @pl.when(block == 0)
    def _():
        for half in range(2):
            for pair in range(pairs):
                start = (2 * pair + (core_ref[0] ^ half)) * chunk
                table_ref[pl.ds((half * pairs + pair) * chunk, chunk), :] = remote_ref[
                    pl.ds(pl.multiple_of(start, 16), chunk), :
                ]

    rows, width = out_ref.shape
    total = mm(near_ref[...], feats_ref[...]) + mm(far_ref[...], table_ref[...])
    degree = jnp.sum(deg_ref[...], axis=1, keepdims=True)
    inverse = 1.0 / jnp.maximum(degree, 1.0)
    mean = (total * inverse).astype(jnp.bfloat16)
    mine = feats_ref[pl.ds(pl.multiple_of(block * rows, rows), rows), :]
    pre = mm(mine, ws_ref[...]) + mm(mean, wn_ref[...])
    sig = jax.nn.sigmoid(pre)
    out_ref[...] = (pre * sig).astype(jnp.bfloat16)
    slope = sig * (1.0 + pre * (1.0 - sig))
    g = (cot_ref[...].astype(jnp.float32) * slope).astype(jnp.bfloat16)
    g_ref[...] = g
    dmsg_ref[...] = (outer_nt(g, wn_ref[...]) * inverse).astype(jnp.bfloat16)

    @pl.when(block == 0)
    def _():
        grads_ref[...] = jnp.zeros_like(grads_ref)

    grads_ref[:width, :] += outer_tn(mine, g)
    grads_ref[width:, :] += outer_tn(mean, g)


def far_kernel(adj_ref, dmsg_ref, *refs):
    back_ref = refs[-1]
    back_ref[...] = outer_tn(adj_ref[...], dmsg_ref[...]).astype(jnp.bfloat16)


def own_kernel(adj_ref, dmsg_ref, g_ref, ws_ref, *refs):
    base_ref = refs[-1]
    base_ref[...] = outer_tn(adj_ref[...], dmsg_ref[...]) + outer_nt(g_ref[...], ws_ref[...])


def finish_kernel(index_ref, base_ref, back_ref, out_ref):
    block = pl.program_id(0)
    rows = out_ref.shape[0]
    far = index_ref.shape[1]
    spot = jnp.clip(index_ref[...] - block * rows, -1, rows).astype(jnp.int16)
    ids = lax.broadcasted_iota(jnp.int16, (rows, far), 0)
    pick = jnp.where(
        ids == jnp.broadcast_to(spot, (rows, far)),
        jnp.ones((rows, far), jnp.bfloat16),
        jnp.zeros((rows, far), jnp.bfloat16),
    )
    out_ref[...] = (base_ref[...] + mm(pick, back_ref[...])).astype(jnp.bfloat16)


def gather_kernel(hub_ref, send_ref, feats_ref, out_ref, wide_ref, *, devices):
    hub_dev = hub_ref.shape[0]
    cap = send_ref.shape[0] // devices
    pack = hub_dev + cap
    wide_ref[...] = feats_ref[...].astype(jnp.float32)

    def rows(index_ref, start):
        picked = [wide_ref[pl.ds(index_ref[start + i], 1), :] for i in range(PACKED)]
        return jnp.concatenate(picked, axis=0).astype(jnp.bfloat16)

    hubs = jnp.concatenate([rows(hub_ref, i) for i in range(0, hub_dev, PACKED)], axis=0)

    def place(p, carry):
        at = pl.multiple_of(p * pack, PACKED)
        out_ref[pl.ds(at, hub_dev), :] = hubs
        for i in range(0, cap, PACKED):
            out_ref[pl.ds(at + hub_dev + i, PACKED), :] = rows(send_ref, p * cap + i)
        return carry

    lax.fori_loop(0, devices, place, 0, unroll=4)


def tie(*arrays):
    return lax.optimization_barrier(arrays)


def call(kernel, grid, in_specs, out_specs, out_shape, name, vmem, aliases=None):
    return pl.pallas_call(
        kernel,
        name=name,
        input_output_aliases=aliases or {},
        grid=grid,
        in_specs=in_specs,
        out_specs=out_specs,
        out_shape=out_shape,
        compiler_params=pltpu.CompilerParams(
            dimension_semantics=("arbitrary",), vmem_limit_bytes=vmem
        ),
    )


def body(feats, w_self, w_neigh, cotangent, hub_rows, send_rows, edge_src, edge_dst):
    devices = lax.axis_size("dom") * lax.axis_size("sub")
    vcount, width = feats.shape
    edges = edge_src.shape[0]
    hub_dev = hub_rows.shape[0]
    cap = send_rows.shape[0] // devices
    pack = hub_dev + cap
    far = devices * pack
    slots = vcount + far
    own_tiles = vcount // T
    all_tiles = slots // T
    tiles = own_tiles * all_tiles
    key_rows = edges // LANES
    f32 = jnp.float32
    bf16 = jnp.bfloat16

    send_table = send_rows.reshape(devices, cap)
    outgoing = pl.pallas_call(
        functools.partial(gather_kernel, devices=devices),
        name="gather",
        out_shape=jax.ShapeDtypeStruct((far, width), bf16),
        grid_spec=pltpu.PrefetchScalarGridSpec(
            num_scalar_prefetch=2,
            grid=(1,),
            in_specs=[pl.BlockSpec((vcount, width), lambda b, *_: (0, 0))],
            out_specs=pl.BlockSpec((far, width), lambda b, *_: (0, 0)),
            scratch_shapes=[pltpu.VMEM((vcount, width), f32)],
        ),
        compiler_params=pltpu.CompilerParams(
            dimension_semantics=("arbitrary",),
            vmem_limit_bytes=(4 << 20) + width * (8 * vcount + 8 * far),
        ),
    )(
        pltpu.with_memory_space_constraint(hub_rows, pltpu.HBM),
        pltpu.with_memory_space_constraint(send_rows, pltpu.HBM),
        pltpu.with_memory_space_constraint(feats, pltpu.HBM),
    ).reshape(devices, pack, width)
    remote = lax.all_to_all(outgoing, AXES, split_axis=0, concat_axis=0, tiled=True)
    remote = remote.reshape(far, width)

    hub_at = edge_src - vcount
    halo_at = hub_at - devices * hub_dev
    dom = lax.axis_size("dom")
    sub = lax.axis_size("sub")
    core = lax.axis_index("dom") % 2

    def place(device):
        d = lax.div(device, sub)
        return (((d ^ core) & 1) * (dom // 2) + (d >> 1)) * sub + lax.rem(device, sub)

    hub_slot = vcount + place(lax.div(hub_at, hub_dev)) * pack + lax.rem(hub_at, hub_dev)
    halo_slot = vcount + place(lax.div(halo_at, cap)) * pack + hub_dev + lax.rem(halo_at, cap)
    slot = jnp.where(hub_at < 0, edge_src, jnp.where(halo_at < 0, hub_slot, halo_slot))
    tile_id = (edge_dst >> 8) * all_tiles + (slot >> 8)
    key = (tile_id << 16) | ((edge_dst & 255) << 8) | (slot & 255)
    keys = lax.sort(key, is_stable=False).reshape(key_rows, LANES)
    heads = keys[:, 0]
    limits = jnp.arange(tiles + 1, dtype=jnp.int32) * (T * T)
    below = jnp.sum((heads[None, :] < limits[:, None]).astype(jnp.int32), axis=1)
    first = jnp.maximum(below[:-1] - 1, 0)
    last = below[1:]
    average = edges / tiles
    window = min(key_rows, math.ceil((average + LANES + 2.0 * math.sqrt(average)) / LANES))
    over = (last > jnp.minimum(first, key_rows - window) + window).astype(jnp.int32)
    flags = jnp.max(over.reshape(own_tiles, all_tiles), axis=1)

    near, away, deg = pl.pallas_call(
        functools.partial(
            counts_kernel, own_tiles=own_tiles, all_tiles=all_tiles, window=window
        ),
        name="counts",
        out_shape=(
            pltpu.HBM((vcount, vcount), bf16),
            pltpu.HBM((vcount, far), bf16),
            pltpu.HBM((vcount, LANES), f32),
        ),
        grid_spec=pltpu.PrefetchScalarGridSpec(
            num_scalar_prefetch=3,
            grid=(own_tiles,),
            in_specs=[pl.BlockSpec((key_rows, LANES), lambda b, *_: (0, 0))],
            out_specs=[
                pl.BlockSpec((T, vcount), lambda b, *_: (b, 0)),
                pl.BlockSpec((T, far), lambda b, *_: (b, 0)),
                pl.BlockSpec((T, LANES), lambda b, *_: (b, 0)),
            ],
            scratch_shapes=[pltpu.VMEM((T, T), f32)],
        ),
        compiler_params=pltpu.CompilerParams(
            dimension_semantics=("arbitrary",), vmem_limit_bytes=(8 << 20) + 6 * T * slots
        ),
    )(first, last, flags, keys)

    near = pltpu.with_memory_space_constraint(near, pltpu.HBM)
    away = pltpu.with_memory_space_constraint(away, pltpu.HBM)
    deg = pltpu.with_memory_space_constraint(deg, pltpu.HBM)
    whole = lambda b, *_: (0, 0)
    by_row = lambda b, *_: (b, 0)
    rows = min(2 * T, vcount)
    layer_out, g, dmsg, parts = pl.pallas_call(
        functools.partial(forward_kernel, chunk=sub * pack),
        name="forward",
        grid_spec=pltpu.PrefetchScalarGridSpec(
            num_scalar_prefetch=1,
            grid=(vcount // rows,),
            in_specs=[
                pl.BlockSpec((rows, vcount), by_row),
                pl.BlockSpec((rows, far), by_row),
                pl.BlockSpec((rows, LANES), by_row),
                pl.BlockSpec((vcount, width), whole),
                pl.BlockSpec((far, width), whole),
                pl.BlockSpec((width, width), whole),
                pl.BlockSpec((width, width), whole),
                pl.BlockSpec((rows, width), by_row),
            ],
            out_specs=[
                pl.BlockSpec((rows, width), by_row),
                pl.BlockSpec((rows, width), by_row),
                pl.BlockSpec((rows, width), by_row),
                pl.BlockSpec((2 * width, width), whole),
            ],
            scratch_shapes=[pltpu.VMEM((far, width), bf16)],
        ),
        out_shape=(
            pltpu.HBM((vcount, width), bf16),
            pltpu.HBM((vcount, width), bf16),
            pltpu.HBM((vcount, width), bf16),
            jax.ShapeDtypeStruct((2 * width, width), f32),
        ),
        compiler_params=pltpu.CompilerParams(
            dimension_semantics=("arbitrary",),
            vmem_limit_bytes=(8 << 20) + 4 * rows * slots + 6 * slots * width,
        ),
    )(
        jnp.reshape(core, (1,)).astype(jnp.int32),
        near,
        away,
        deg,
        feats,
        remote,
        w_self,
        w_neigh,
        pltpu.with_memory_space_constraint(cotangent, pltpu.HBM),
    )

    g = pltpu.with_memory_space_constraint(g, pltpu.HBM)
    dmsg = pltpu.with_memory_space_constraint(dmsg, pltpu.HBM)
    half = devices // 2
    twin = [(i, i ^ 1) for i in range(dom)]
    groups = [
        [d * sub + i for d in range(c, dom, 2) for i in range(sub)] for c in range(2)
    ]

    def exchange(x):
        return lax.all_to_all(
            x, AXES, split_axis=0, concat_axis=0, axis_index_groups=groups, tiled=True
        )

    far_cols = max(c for c in range(T, 4 * T, T) if far // 2 % c == 0)
    far_steps = far // 2 // far_cols

    def far_part(side, dmsg):
        return call(
            far_kernel,
            (far_steps,),
            [
                pl.BlockSpec((vcount, far_cols), lambda j: (0, j + side * far_steps)),
                pl.BlockSpec((vcount, width), whole),
            ],
            pl.BlockSpec((far_cols, width), by_row),
            jax.ShapeDtypeStruct((far // 2, width), bf16),
            "far",
            24 << 20,
        )(away, dmsg)

    sent = lax.dynamic_slice_in_dim(parts, (1 - core) * width, width, 0)
    kept = lax.dynamic_slice_in_dim(parts, core * width, width, 0)
    came = lax.ppermute(sent, "dom", twin)
    given = far_part(1, dmsg)
    got = lax.ppermute(given, "dom", twin)
    dmsg, given = tie(dmsg, given)
    kept_slots = far_part(0, dmsg)
    came, kept_slots = tie(came, kept_slots)
    share = width // half
    piece = (kept + came).astype(bf16).reshape(half, share, width)
    kept_slots = kept_slots.reshape(half, pack, width)
    got = got.reshape(half, pack, width)
    hub_sum = kept_slots[:, :hub_dev].astype(f32) + got[:, :hub_dev].astype(f32)
    payload = jnp.concatenate(
        [hub_sum.astype(bf16), kept_slots[:, hub_dev:], got[:, hub_dev:], piece], axis=1
    )
    bundle = payload.shape[1]
    returned = exchange(payload)
    cols = 2 * T
    base = call(
        own_kernel,
        (vcount // cols,),
        [
            pl.BlockSpec((vcount, cols), lambda j: (0, j)),
            pl.BlockSpec((vcount, width), whole),
            pl.BlockSpec((cols, width), by_row),
            pl.BlockSpec((width, width), whole),
        ],
        pl.BlockSpec((cols, width), by_row),
        jax.ShapeDtypeStruct((vcount, width), f32),
        "own",
        16 << 20,
    )(near, dmsg, g, w_self)

    mine = jnp.sum(returned[:, bundle - share :].astype(f32), axis=0).astype(bf16)
    mine, base = tie(mine, base)
    mine = exchange(jnp.broadcast_to(mine[None], (half, share, width))).reshape(width, width)
    table = send_rows.reshape(dom // 2, 2, sub, cap)
    same = lax.dynamic_index_in_dim(table, core, 1, keepdims=False).reshape(half, cap)
    cross = lax.dynamic_index_in_dim(table, 1 - core, 1, keepdims=False).reshape(half, cap)
    index = jnp.concatenate(
        [
            jnp.broadcast_to(hub_rows[None], (half, hub_dev)),
            same,
            cross,
            jnp.full((half, share), -1, jnp.int32),
        ],
        axis=1,
    ).reshape(1, half * bundle)
    grad_feats = call(
        finish_kernel,
        (vcount // rows,),
        [
            pl.BlockSpec((1, half * bundle), whole),
            pl.BlockSpec((rows, width), by_row),
            pl.BlockSpec((half * bundle, width), whole),
        ],
        pl.BlockSpec((rows, width), by_row),
        jax.ShapeDtypeStruct((vcount, width), bf16),
        "finish",
        (8 << 20) + 8 * far * width,
    )(index, base, returned.reshape(half * bundle, width))
    mine, grad_feats = tie(mine, grad_feats)
    other = lax.ppermute(mine, "dom", twin)
    grad_self = jnp.where(core == 0, mine, other).astype(f32)
    grad_neigh = jnp.where(core == 0, other, mine).astype(f32)
    return (layer_out, grad_feats, grad_self, grad_neigh)


def solution(mesh):
    return jax.shard_map(
        body,
        mesh=mesh,
        in_specs=(
            P(AXES, None),
            P(),
            P(),
            P(AXES, None),
            P(AXES),
            P(AXES),
            P(AXES),
            P(AXES),
        ),
        out_specs=(P(AXES, None), P(AXES, None), P(), P()),
        check_vma=False,
    )
```

```python
import functools
import math

import jax
import jax.numpy as jnp
from jax import lax
from jax.experimental import pallas as pl
from jax.experimental.pallas import tpu as pltpu
from jax.sharding import PartitionSpec as P

AXES = ("dom", "sub")
T = 256
LANES = 128
PACKED = 16
F8 = jnp.float8_e4m3fn


def outer_nt(a, b):
    return lax.dot_general(a, b, (((1,), (1,)), ((), ())), preferred_element_type=jnp.float32)


def outer_tn(a, b):
    return lax.dot_general(a, b, (((0,), (0,)), ((), ())), preferred_element_type=jnp.float32)


def mm(a, b):
    return jnp.dot(a, b, preferred_element_type=jnp.float32)


def counts_kernel(first_ref, last_ref, flag_ref, keys_ref, near_ref, far_ref, deg_ref, tile_ref,
                  *, own_tiles, all_tiles, window):
    block = pl.program_id(0)
    key_rows = keys_ref.shape[0]
    ids = (lax.broadcasted_iota(jnp.int32, (T, LANES), 0) - 128).astype(jnp.int8)
    none = jnp.zeros((T, LANES), F8)
    ones = jnp.ones((T, LANES), F8)

    def match(low):
        return ids == jnp.broadcast_to((low - 128).astype(jnp.int8), (T, LANES))

    def tile_part(tile, row, count):
        left = []
        right = []
        for q in range(count):
            keys = keys_ref[pl.ds(row + q, 1), :]
            inside = jnp.where((keys >> 16) == tile, 1.0, 0.0).astype(F8)
            left.append(
                jnp.where(match((keys >> 8) & 255), jnp.broadcast_to(inside, (T, LANES)), none)
            )
            right.append(jnp.where(match(keys & 255), ones, none))
        return outer_nt(jnp.concatenate(left, axis=1), jnp.concatenate(right, axis=1))

    deg_ref[...] = jnp.zeros_like(deg_ref)

    ranges = [(near_ref, 0, own_tiles), (far_ref, own_tiles, all_tiles - own_tiles)]

    for ref, shift, number in ranges:

        def build(j, carry, ref=ref, shift=shift):
            tile = block * all_tiles + shift + j
            start = jnp.minimum(first_ref[tile], key_rows - window)
            counts = tile_part(tile, start, window)
            deg_ref[...] += counts[:, :LANES] + counts[:, LANES:]
            ref[:, pl.ds(pl.multiple_of(j * T, T), T)] = counts.astype(jnp.bfloat16)
            return carry

        unroll = max(u for u in range(1, 13) if number % u == 0)
        lax.fori_loop(0, number, build, 0, unroll=unroll)

    @pl.when(flag_ref[block] > 0)
    def _():
        for ref, shift, number in ranges:

            def rest(j, carry, ref=ref, shift=shift):
                tile = block * all_tiles + shift + j
                start = jnp.minimum(first_ref[tile], key_rows - window)
                stop = last_ref[tile]

                @pl.when(stop > start + window)
                def _():
                    tile_ref[...] = tile_part(tile, start, window)

                    def more(row, inner):
                        counts = tile_part(tile, row, 1)
                        deg_ref[...] += counts[:, :LANES] + counts[:, LANES:]
                        tile_ref[...] += counts
                        return inner

                    lax.fori_loop(start + window, stop, more, 0)
                    cols = pl.ds(pl.multiple_of(j * T, T), T)
                    ref[:, cols] = tile_ref[...].astype(jnp.bfloat16)

                return carry

            lax.fori_loop(0, number, rest, 0)


def forward_kernel(core_ref, near_ref, far_ref, deg_ref, feats_ref, remote_ref, ws_ref, wn_ref, cot_ref,
                   out_ref, g_ref, dmsg_ref, grads_ref, table_ref, *, chunk):
    block = pl.program_id(0)
    pairs = remote_ref.shape[0] // chunk // 2

    @pl.when(block == 0)
    def _():
        grads_ref[...] = jnp.zeros_like(grads_ref)
        for half in range(2):
            for pair in range(pairs):
                start = (2 * pair + (core_ref[0] ^ half)) * chunk
                table_ref[pl.ds((half * pairs + pair) * chunk, chunk), :] = remote_ref[
                    pl.ds(pl.multiple_of(start, 16), chunk), :
                ]

    rows, width = out_ref.shape
    total = mm(near_ref[...], feats_ref[...]) + mm(far_ref[...], table_ref[...])
    degree = jnp.sum(deg_ref[...], axis=1, keepdims=True)
    inverse = 1.0 / jnp.maximum(degree, 1.0)
    mean = (total * inverse).astype(jnp.bfloat16)
    mine = feats_ref[pl.ds(pl.multiple_of(block * rows, rows), rows), :]
    pre = mm(mine, ws_ref[...]) + mm(mean, wn_ref[...])
    sig = jax.nn.sigmoid(pre)
    out_ref[...] = (pre * sig).astype(jnp.bfloat16)
    slope = sig * (1.0 + pre * (1.0 - sig))
    g = (cot_ref[...].astype(jnp.float32) * slope).astype(jnp.bfloat16)
    g_ref[...] = g
    dmsg_ref[...] = (outer_nt(g, wn_ref[...]) * inverse).astype(jnp.bfloat16)

    grads_ref[:width, :] += outer_tn(mine, g)
    grads_ref[width:, :] += outer_tn(mean, g)


def far_kernel(adj_ref, dmsg_ref, *refs):
    back_ref = refs[-1]
    back_ref[...] = outer_tn(adj_ref[...], dmsg_ref[...]).astype(jnp.bfloat16)


def own_kernel(adj_ref, dmsg_ref, g_ref, ws_ref, *refs):
    base_ref = refs[-1]
    base_ref[...] = outer_tn(adj_ref[...], dmsg_ref[...]) + outer_nt(g_ref[...], ws_ref[...])


def finish_kernel(index_ref, base_ref, back_ref, out_ref):
    block = pl.program_id(0)
    rows = out_ref.shape[0]
    far = index_ref.shape[1]
    spot = jnp.clip(index_ref[...] - block * rows, -1, rows).astype(jnp.int16)
    ids = lax.broadcasted_iota(jnp.int16, (rows, far), 0)
    pick = jnp.where(
        ids == jnp.broadcast_to(spot, (rows, far)),
        jnp.ones((rows, far), jnp.bfloat16),
        jnp.zeros((rows, far), jnp.bfloat16),
    )
    out_ref[...] = (base_ref[...] + mm(pick, back_ref[...])).astype(jnp.bfloat16)


def gather_kernel(hub_ref, send_ref, feats_ref, out_ref, wide_ref, *, devices):
    hub_dev = hub_ref.shape[0]
    cap = send_ref.shape[0] // devices
    pack = hub_dev + cap
    wide_ref[...] = feats_ref[...].astype(jnp.float32)

    def rows(index_ref, start):
        picked = [wide_ref[pl.ds(index_ref[start + i], 1), :] for i in range(PACKED)]
        return jnp.concatenate(picked, axis=0).astype(jnp.bfloat16)

    hubs = jnp.concatenate([rows(hub_ref, i) for i in range(0, hub_dev, PACKED)], axis=0)

    def place(p, carry):
        at = pl.multiple_of(p * pack, PACKED)
        out_ref[pl.ds(at, hub_dev), :] = hubs
        for i in range(0, cap, PACKED):
            out_ref[pl.ds(at + hub_dev + i, PACKED), :] = rows(send_ref, p * cap + i)
        return carry

    lax.fori_loop(0, devices, place, 0, unroll=4)


def tie(*arrays):
    return lax.optimization_barrier(arrays)


def call(kernel, grid, in_specs, out_specs, out_shape, name, vmem, aliases=None):
    return pl.pallas_call(
        kernel,
        name=name,
        input_output_aliases=aliases or {},
        grid=grid,
        in_specs=in_specs,
        out_specs=out_specs,
        out_shape=out_shape,
        compiler_params=pltpu.CompilerParams(
            dimension_semantics=("arbitrary",), vmem_limit_bytes=vmem
        ),
    )


def body(feats, w_self, w_neigh, cotangent, hub_rows, send_rows, edge_src, edge_dst):
    devices = lax.axis_size("dom") * lax.axis_size("sub")
    vcount, width = feats.shape
    edges = edge_src.shape[0]
    hub_dev = hub_rows.shape[0]
    cap = send_rows.shape[0] // devices
    pack = hub_dev + cap
    far = devices * pack
    slots = vcount + far
    own_tiles = vcount // T
    all_tiles = slots // T
    tiles = own_tiles * all_tiles
    key_rows = edges // LANES
    f32 = jnp.float32
    bf16 = jnp.bfloat16

    send_table = send_rows.reshape(devices, cap)
    outgoing = pl.pallas_call(
        functools.partial(gather_kernel, devices=devices),
        name="gather",
        out_shape=jax.ShapeDtypeStruct((far, width), bf16),
        grid_spec=pltpu.PrefetchScalarGridSpec(
            num_scalar_prefetch=2,
            grid=(1,),
            in_specs=[pl.BlockSpec((vcount, width), lambda b, *_: (0, 0))],
            out_specs=pl.BlockSpec((far, width), lambda b, *_: (0, 0)),
            scratch_shapes=[pltpu.VMEM((vcount, width), f32)],
        ),
        compiler_params=pltpu.CompilerParams(
            dimension_semantics=("arbitrary",),
            vmem_limit_bytes=(4 << 20) + width * (8 * vcount + 8 * far),
        ),
    )(
        pltpu.with_memory_space_constraint(hub_rows, pltpu.HBM),
        pltpu.with_memory_space_constraint(send_rows, pltpu.HBM),
        pltpu.with_memory_space_constraint(feats, pltpu.HBM),
    ).reshape(devices, pack, width)
    remote = lax.all_to_all(outgoing, AXES, split_axis=0, concat_axis=0, tiled=True)
    remote = remote.reshape(far, width)

    hub_at = edge_src - vcount
    halo_at = hub_at - devices * hub_dev
    dom = lax.axis_size("dom")
    sub = lax.axis_size("sub")
    core = lax.axis_index("dom") % 2

    def place(device):
        d = lax.div(device, sub)
        return (((d ^ core) & 1) * (dom // 2) + (d >> 1)) * sub + lax.rem(device, sub)

    hub_slot = vcount + place(lax.div(hub_at, hub_dev)) * pack + lax.rem(hub_at, hub_dev)
    halo_slot = vcount + place(lax.div(halo_at, cap)) * pack + hub_dev + lax.rem(halo_at, cap)
    slot = jnp.where(hub_at < 0, edge_src, jnp.where(halo_at < 0, hub_slot, halo_slot))
    tile_id = (edge_dst >> 8) * all_tiles + (slot >> 8)
    key = (tile_id << 16) | ((edge_dst & 255) << 8) | (slot & 255)
    keys = lax.sort(key, is_stable=False).reshape(key_rows, LANES)
    heads = keys[:, 0]
    limits = jnp.arange(tiles + 1, dtype=jnp.int32) * (T * T)
    below = jnp.sum((heads[None, :] < limits[:, None]).astype(jnp.int32), axis=1)
    first = jnp.maximum(below[:-1] - 1, 0)
    last = below[1:]
    average = edges / tiles
    window = min(key_rows, math.ceil((average + LANES + 2.0 * math.sqrt(average)) / LANES))
    over = (last > jnp.minimum(first, key_rows - window) + window).astype(jnp.int32)
    flags = jnp.max(over.reshape(own_tiles, all_tiles), axis=1)

    near, away, deg = pl.pallas_call(
        functools.partial(
            counts_kernel, own_tiles=own_tiles, all_tiles=all_tiles, window=window
        ),
        name="counts",
        out_shape=(
            pltpu.HBM((vcount, vcount), bf16),
            pltpu.HBM((vcount, far), bf16),
            pltpu.HBM((vcount, LANES), f32),
        ),
        grid_spec=pltpu.PrefetchScalarGridSpec(
            num_scalar_prefetch=3,
            grid=(own_tiles,),
            in_specs=[pl.BlockSpec((key_rows, LANES), lambda b, *_: (0, 0))],
            out_specs=[
                pl.BlockSpec((T, vcount), lambda b, *_: (b, 0)),
                pl.BlockSpec((T, far), lambda b, *_: (b, 0)),
                pl.BlockSpec((T, LANES), lambda b, *_: (b, 0)),
            ],
            scratch_shapes=[pltpu.VMEM((T, T), f32)],
        ),
        compiler_params=pltpu.CompilerParams(
            dimension_semantics=("arbitrary",), vmem_limit_bytes=(8 << 20) + 6 * T * slots
        ),
    )(first, last, flags, keys)

    near = pltpu.with_memory_space_constraint(near, pltpu.HBM)
    away = pltpu.with_memory_space_constraint(away, pltpu.HBM)
    deg = pltpu.with_memory_space_constraint(deg, pltpu.HBM)
    whole = lambda b, *_: (0, 0)
    by_row = lambda b, *_: (b, 0)
    rows = min(2 * T, vcount)
    layer_out, g, dmsg, parts = pl.pallas_call(
        functools.partial(forward_kernel, chunk=sub * pack),
        name="forward",
        grid_spec=pltpu.PrefetchScalarGridSpec(
            num_scalar_prefetch=1,
            grid=(vcount // rows,),
            in_specs=[
                pl.BlockSpec((rows, vcount), by_row),
                pl.BlockSpec((rows, far), by_row),
                pl.BlockSpec((rows, LANES), by_row),
                pl.BlockSpec((vcount, width), whole),
                pl.BlockSpec((far, width), whole),
                pl.BlockSpec((width, width), whole),
                pl.BlockSpec((width, width), whole),
                pl.BlockSpec((rows, width), by_row),
            ],
            out_specs=[
                pl.BlockSpec((rows, width), by_row),
                pl.BlockSpec((rows, width), by_row),
                pl.BlockSpec((rows, width), by_row),
                pl.BlockSpec((2 * width, width), whole),
            ],
            scratch_shapes=[pltpu.VMEM((far, width), bf16)],
        ),
        out_shape=(
            pltpu.HBM((vcount, width), bf16),
            pltpu.HBM((vcount, width), bf16),
            pltpu.HBM((vcount, width), bf16),
            jax.ShapeDtypeStruct((2 * width, width), f32),
        ),
        compiler_params=pltpu.CompilerParams(
            dimension_semantics=("arbitrary",),
            vmem_limit_bytes=(8 << 20) + 4 * rows * slots + 6 * slots * width,
        ),
    )(
        jnp.reshape(core, (1,)).astype(jnp.int32),
        near,
        away,
        deg,
        feats,
        remote,
        w_self,
        w_neigh,
        pltpu.with_memory_space_constraint(cotangent, pltpu.HBM),
    )

    g = pltpu.with_memory_space_constraint(g, pltpu.HBM)
    dmsg = pltpu.with_memory_space_constraint(dmsg, pltpu.HBM)
    half = devices // 2
    twin = [(i, i ^ 1) for i in range(dom)]
    groups = [
        [d * sub + i for d in range(c, dom, 2) for i in range(sub)] for c in range(2)
    ]

    def exchange(x):
        return lax.all_to_all(
            x, AXES, split_axis=0, concat_axis=0, axis_index_groups=groups, tiled=True
        )

    far_cols = max(c for c in range(T, 4 * T, T) if far // 2 % c == 0)
    far_steps = far // 2 // far_cols

    def far_part(side, dmsg):
        return call(
            far_kernel,
            (far_steps,),
            [
                pl.BlockSpec((vcount, far_cols), lambda j: (0, j + side * far_steps)),
                pl.BlockSpec((vcount, width), whole),
            ],
            pl.BlockSpec((far_cols, width), by_row),
            jax.ShapeDtypeStruct((far // 2, width), bf16),
            "far",
            24 << 20,
        )(away, dmsg)

    sent = lax.dynamic_slice_in_dim(parts, (1 - core) * width, width, 0)
    kept = lax.dynamic_slice_in_dim(parts, core * width, width, 0)
    came = lax.ppermute(sent, "dom", twin)
    given = far_part(1, dmsg)
    got = lax.ppermute(given, "dom", twin)
    dmsg, given = tie(dmsg, given)
    kept_slots = far_part(0, dmsg)
    came, kept_slots = tie(came, kept_slots)
    share = width // half
    piece = (kept + came).astype(bf16).reshape(half, share, width)
    kept_slots = kept_slots.reshape(half, pack, width)
    got = got.reshape(half, pack, width)
    hub_sum = kept_slots[:, :hub_dev].astype(f32) + got[:, :hub_dev].astype(f32)
    payload = jnp.concatenate(
        [hub_sum.astype(bf16), kept_slots[:, hub_dev:], got[:, hub_dev:], piece], axis=1
    )
    bundle = payload.shape[1]
    returned = exchange(payload)
    cols = 2 * T
    base = call(
        own_kernel,
        (vcount // cols,),
        [
            pl.BlockSpec((vcount, cols), lambda j: (0, j)),
            pl.BlockSpec((vcount, width), whole),
            pl.BlockSpec((cols, width), by_row),
            pl.BlockSpec((width, width), whole),
        ],
        pl.BlockSpec((cols, width), by_row),
        jax.ShapeDtypeStruct((vcount, width), f32),
        "own",
        16 << 20,
    )(near, dmsg, g, w_self)

    mine = jnp.sum(returned[:, bundle - share :].astype(f32), axis=0).astype(bf16)
    mine, base = tie(mine, base)
    mine = exchange(jnp.broadcast_to(mine[None], (half, share, width))).reshape(width, width)
    table = send_rows.reshape(dom // 2, 2, sub, cap)
    same = lax.dynamic_index_in_dim(table, core, 1, keepdims=False).reshape(half, cap)
    cross = lax.dynamic_index_in_dim(table, 1 - core, 1, keepdims=False).reshape(half, cap)
    index = jnp.concatenate(
        [
            jnp.broadcast_to(hub_rows[None], (half, hub_dev)),
            same,
            cross,
            jnp.full((half, share), -1, jnp.int32),
        ],
        axis=1,
    ).reshape(1, half * bundle)
    grad_feats = call(
        finish_kernel,
        (vcount // rows,),
        [
            pl.BlockSpec((1, half * bundle), whole),
            pl.BlockSpec((rows, width), by_row),
            pl.BlockSpec((half * bundle, width), whole),
        ],
        pl.BlockSpec((rows, width), by_row),
        jax.ShapeDtypeStruct((vcount, width), bf16),
        "finish",
        (8 << 20) + 8 * far * width,
    )(index, base, returned.reshape(half * bundle, width))
    mine, grad_feats = tie(mine, grad_feats)
    other = lax.ppermute(mine, "dom", twin)
    grad_self = jnp.where(core == 0, mine, other).astype(f32)
    grad_neigh = jnp.where(core == 0, other, mine).astype(f32)
    return (layer_out, grad_feats, grad_self, grad_neigh)


def solution(mesh):
    return jax.shard_map(
        body,
        mesh=mesh,
        in_specs=(
            P(AXES, None),
            P(),
            P(),
            P(AXES, None),
            P(AXES),
            P(AXES),
            P(AXES),
            P(AXES),
        ),
        out_specs=(P(AXES, None), P(AXES, None), P(), P()),
        check_vma=False,
    )
```

```python
import functools
import math

import jax
import jax.numpy as jnp
from jax import lax
from jax.experimental import pallas as pl
from jax.experimental.pallas import tpu as pltpu
from jax.sharding import PartitionSpec as P

AXES = ("dom", "sub")
T = 256
LANES = 128
PACKED = 16
F8 = jnp.float8_e4m3fn


def outer_nt(a, b):
    return lax.dot_general(a, b, (((1,), (1,)), ((), ())), preferred_element_type=jnp.float32)


def outer_tn(a, b):
    return lax.dot_general(a, b, (((0,), (0,)), ((), ())), preferred_element_type=jnp.float32)


def mm(a, b):
    return jnp.dot(a, b, preferred_element_type=jnp.float32)


def counts_kernel(first_ref, last_ref, flag_ref, keys_ref, near_ref, far_ref, deg_ref, tile_ref,
                  *, own_tiles, all_tiles, window):
    block = pl.program_id(0)
    key_rows = keys_ref.shape[0]
    ids = (lax.broadcasted_iota(jnp.int32, (T, LANES), 0) - 128).astype(jnp.int8)
    none = jnp.zeros((T, LANES), F8)
    ones = jnp.ones((T, LANES), F8)

    def match(low):
        return ids == jnp.broadcast_to((low - 128).astype(jnp.int8), (T, LANES))

    def tile_part(tile, row, count):
        left = []
        right = []
        for q in range(count):
            keys = keys_ref[pl.ds(row + q, 1), :]
            inside = jnp.where((keys >> 16) == tile, 1.0, 0.0).astype(F8)
            left.append(
                jnp.where(match((keys >> 8) & 255), jnp.broadcast_to(inside, (T, LANES)), none)
            )
            right.append(jnp.where(match(keys & 255), ones, none))
        return outer_nt(jnp.concatenate(left, axis=1), jnp.concatenate(right, axis=1))

    deg_ref[...] = jnp.zeros_like(deg_ref)

    ranges = [(near_ref, 0, own_tiles), (far_ref, own_tiles, all_tiles - own_tiles)]

    for ref, shift, number in ranges:

        def build(j, carry, ref=ref, shift=shift):
            tile = block * all_tiles + shift + j
            start = jnp.minimum(first_ref[tile], key_rows - window)
            counts = tile_part(tile, start, window)
            deg_ref[...] += counts[:, :LANES] + counts[:, LANES:]
            ref[:, pl.ds(pl.multiple_of(j * T, T), T)] = counts.astype(jnp.bfloat16)
            return carry

        unroll = max(u for u in range(1, 13) if number % u == 0)
        lax.fori_loop(0, number, build, 0, unroll=unroll)

    @pl.when(flag_ref[block] > 0)
    def _():
        for ref, shift, number in ranges:

            def rest(j, carry, ref=ref, shift=shift):
                tile = block * all_tiles + shift + j
                start = jnp.minimum(first_ref[tile], key_rows - window)
                stop = last_ref[tile]

                @pl.when(stop > start + window)
                def _():
                    tile_ref[...] = tile_part(tile, start, window)

                    def more(row, inner):
                        counts = tile_part(tile, row, 1)
                        deg_ref[...] += counts[:, :LANES] + counts[:, LANES:]
                        tile_ref[...] += counts
                        return inner

                    lax.fori_loop(start + window, stop, more, 0)
                    cols = pl.ds(pl.multiple_of(j * T, T), T)
                    ref[:, cols] = tile_ref[...].astype(jnp.bfloat16)

                return carry

            lax.fori_loop(0, number, rest, 0)


def forward_kernel(core_ref, near_ref, far_ref, deg_ref, feats_ref, remote_ref, ws_ref, wn_ref, cot_ref,
                   out_ref, g_ref, dmsg_ref, grads_ref, table_ref, *, chunk):
    block = pl.program_id(0)
    pairs = remote_ref.shape[0] // chunk // 2

    @pl.when(block == 0)
    def _():
        grads_ref[...] = jnp.zeros_like(grads_ref)
        for half in range(2):
            for pair in range(pairs):
                start = (2 * pair + (core_ref[0] ^ half)) * chunk
                table_ref[pl.ds((half * pairs + pair) * chunk, chunk), :] = remote_ref[
                    pl.ds(pl.multiple_of(start, 16), chunk), :
                ]

    rows = out_ref.shape[0]
    total = mm(near_ref[...], feats_ref[...]) + mm(far_ref[...], table_ref[...])
    degree = jnp.sum(deg_ref[...], axis=1, keepdims=True)
    inverse = 1.0 / jnp.maximum(degree, 1.0)
    mean = (total * inverse).astype(jnp.bfloat16)
    mine = feats_ref[pl.ds(pl.multiple_of(block * rows, rows), rows), :]
    both = jnp.concatenate([mine, mean], axis=1)
    pre = mm(both, jnp.concatenate([ws_ref[...], wn_ref[...]], axis=0))
    sig = jax.nn.sigmoid(pre)
    out_ref[...] = (pre * sig).astype(jnp.bfloat16)
    slope = sig * (1.0 + pre * (1.0 - sig))
    g = (cot_ref[...].astype(jnp.float32) * slope).astype(jnp.bfloat16)
    g_ref[...] = g
    dmsg_ref[...] = (outer_nt(g, wn_ref[...]) * inverse).astype(jnp.bfloat16)

    grads_ref[...] += outer_tn(both, g)


def far_kernel(adj_ref, dmsg_ref, *refs):
    back_ref = refs[-1]
    back_ref[...] = outer_tn(adj_ref[...], dmsg_ref[...]).astype(jnp.bfloat16)


def own_kernel(adj_ref, dmsg_ref, g_ref, ws_ref, *refs):
    base_ref = refs[-1]
    base_ref[...] = outer_tn(adj_ref[...], dmsg_ref[...]) + outer_nt(g_ref[...], ws_ref[...])


def finish_kernel(index_ref, base_ref, back_ref, out_ref):
    block = pl.program_id(0)
    rows = out_ref.shape[0]
    far = index_ref.shape[1]
    spot = jnp.clip(index_ref[...] - block * rows, -1, rows).astype(jnp.int16)
    ids = lax.broadcasted_iota(jnp.int16, (rows, far), 0)
    pick = jnp.where(
        ids == jnp.broadcast_to(spot, (rows, far)),
        jnp.ones((rows, far), jnp.bfloat16),
        jnp.zeros((rows, far), jnp.bfloat16),
    )
    out_ref[...] = (base_ref[...] + mm(pick, back_ref[...])).astype(jnp.bfloat16)


def gather_kernel(hub_ref, send_ref, feats_ref, out_ref, wide_ref, *, devices):
    hub_dev = hub_ref.shape[0]
    cap = send_ref.shape[0] // devices
    pack = hub_dev + cap
    wide_ref[...] = feats_ref[...].astype(jnp.float32)

    def rows(index_ref, start):
        picked = [wide_ref[pl.ds(index_ref[start + i], 1), :] for i in range(PACKED)]
        return jnp.concatenate(picked, axis=0).astype(jnp.bfloat16)

    hubs = jnp.concatenate([rows(hub_ref, i) for i in range(0, hub_dev, PACKED)], axis=0)

    def place(p, carry):
        at = pl.multiple_of(p * pack, PACKED)
        out_ref[pl.ds(at, hub_dev), :] = hubs
        for i in range(0, cap, PACKED):
            out_ref[pl.ds(at + hub_dev + i, PACKED), :] = rows(send_ref, p * cap + i)
        return carry

    lax.fori_loop(0, devices, place, 0, unroll=4)


def tie(*arrays):
    return lax.optimization_barrier(arrays)


def call(kernel, grid, in_specs, out_specs, out_shape, name, vmem, aliases=None):
    return pl.pallas_call(
        kernel,
        name=name,
        input_output_aliases=aliases or {},
        grid=grid,
        in_specs=in_specs,
        out_specs=out_specs,
        out_shape=out_shape,
        compiler_params=pltpu.CompilerParams(
            dimension_semantics=("arbitrary",), vmem_limit_bytes=vmem
        ),
    )


def body(feats, w_self, w_neigh, cotangent, hub_rows, send_rows, edge_src, edge_dst):
    devices = lax.axis_size("dom") * lax.axis_size("sub")
    vcount, width = feats.shape
    edges = edge_src.shape[0]
    hub_dev = hub_rows.shape[0]
    cap = send_rows.shape[0] // devices
    pack = hub_dev + cap
    far = devices * pack
    slots = vcount + far
    own_tiles = vcount // T
    all_tiles = slots // T
    tiles = own_tiles * all_tiles
    key_rows = edges // LANES
    f32 = jnp.float32
    bf16 = jnp.bfloat16

    send_table = send_rows.reshape(devices, cap)
    outgoing = pl.pallas_call(
        functools.partial(gather_kernel, devices=devices),
        name="gather",
        out_shape=jax.ShapeDtypeStruct((far, width), bf16),
        grid_spec=pltpu.PrefetchScalarGridSpec(
            num_scalar_prefetch=2,
            grid=(1,),
            in_specs=[pl.BlockSpec((vcount, width), lambda b, *_: (0, 0))],
            out_specs=pl.BlockSpec((far, width), lambda b, *_: (0, 0)),
            scratch_shapes=[pltpu.VMEM((vcount, width), f32)],
        ),
        compiler_params=pltpu.CompilerParams(
            dimension_semantics=("arbitrary",),
            vmem_limit_bytes=(4 << 20) + width * (8 * vcount + 8 * far),
        ),
    )(
        pltpu.with_memory_space_constraint(hub_rows, pltpu.HBM),
        pltpu.with_memory_space_constraint(send_rows, pltpu.HBM),
        pltpu.with_memory_space_constraint(feats, pltpu.HBM),
    ).reshape(devices, pack, width)
    remote = lax.all_to_all(outgoing, AXES, split_axis=0, concat_axis=0, tiled=True)
    remote = remote.reshape(far, width)

    hub_at = edge_src - vcount
    halo_at = hub_at - devices * hub_dev
    dom = lax.axis_size("dom")
    sub = lax.axis_size("sub")
    core = lax.axis_index("dom") % 2

    def place(device):
        d = lax.div(device, sub)
        return (((d ^ core) & 1) * (dom // 2) + (d >> 1)) * sub + lax.rem(device, sub)

    hub_slot = vcount + place(lax.div(hub_at, hub_dev)) * pack + lax.rem(hub_at, hub_dev)
    halo_slot = vcount + place(lax.div(halo_at, cap)) * pack + hub_dev + lax.rem(halo_at, cap)
    slot = jnp.where(hub_at < 0, edge_src, jnp.where(halo_at < 0, hub_slot, halo_slot))
    tile_id = (edge_dst >> 8) * all_tiles + (slot >> 8)
    key = (tile_id << 16) | ((edge_dst & 255) << 8) | (slot & 255)
    keys = lax.sort(key, is_stable=False).reshape(key_rows, LANES)
    heads = keys[:, 0]
    limits = jnp.arange(tiles + 1, dtype=jnp.int32) * (T * T)
    below = jnp.sum((heads[None, :] < limits[:, None]).astype(jnp.int32), axis=1)
    first = jnp.maximum(below[:-1] - 1, 0)
    last = below[1:]
    average = edges / tiles
    window = min(key_rows, math.ceil((average + LANES + 2.0 * math.sqrt(average)) / LANES))
    over = (last > jnp.minimum(first, key_rows - window) + window).astype(jnp.int32)
    flags = jnp.max(over.reshape(own_tiles, all_tiles), axis=1)

    near, away, deg = pl.pallas_call(
        functools.partial(
            counts_kernel, own_tiles=own_tiles, all_tiles=all_tiles, window=window
        ),
        name="counts",
        out_shape=(
            pltpu.HBM((vcount, vcount), bf16),
            pltpu.HBM((vcount, far), bf16),
            pltpu.HBM((vcount, LANES), f32),
        ),
        grid_spec=pltpu.PrefetchScalarGridSpec(
            num_scalar_prefetch=3,
            grid=(own_tiles,),
            in_specs=[pl.BlockSpec((key_rows, LANES), lambda b, *_: (0, 0))],
            out_specs=[
                pl.BlockSpec((T, vcount), lambda b, *_: (b, 0)),
                pl.BlockSpec((T, far), lambda b, *_: (b, 0)),
                pl.BlockSpec((T, LANES), lambda b, *_: (b, 0)),
            ],
            scratch_shapes=[pltpu.VMEM((T, T), f32)],
        ),
        compiler_params=pltpu.CompilerParams(
            dimension_semantics=("arbitrary",), vmem_limit_bytes=(8 << 20) + 6 * T * slots
        ),
    )(first, last, flags, keys)

    near = pltpu.with_memory_space_constraint(near, pltpu.HBM)
    away = pltpu.with_memory_space_constraint(away, pltpu.HBM)
    deg = pltpu.with_memory_space_constraint(deg, pltpu.HBM)
    whole = lambda b, *_: (0, 0)
    by_row = lambda b, *_: (b, 0)
    rows = min(2 * T, vcount)
    layer_out, g, dmsg, parts = pl.pallas_call(
        functools.partial(forward_kernel, chunk=sub * pack),
        name="forward",
        grid_spec=pltpu.PrefetchScalarGridSpec(
            num_scalar_prefetch=1,
            grid=(vcount // rows,),
            in_specs=[
                pl.BlockSpec((rows, vcount), by_row),
                pl.BlockSpec((rows, far), by_row),
                pl.BlockSpec((rows, LANES), by_row),
                pl.BlockSpec((vcount, width), whole),
                pl.BlockSpec((far, width), whole),
                pl.BlockSpec((width, width), whole),
                pl.BlockSpec((width, width), whole),
                pl.BlockSpec((rows, width), by_row),
            ],
            out_specs=[
                pl.BlockSpec((rows, width), by_row),
                pl.BlockSpec((rows, width), by_row),
                pl.BlockSpec((rows, width), by_row),
                pl.BlockSpec((2 * width, width), whole),
            ],
            scratch_shapes=[pltpu.VMEM((far, width), bf16)],
        ),
        out_shape=(
            pltpu.HBM((vcount, width), bf16),
            pltpu.HBM((vcount, width), bf16),
            pltpu.HBM((vcount, width), bf16),
            jax.ShapeDtypeStruct((2 * width, width), f32),
        ),
        compiler_params=pltpu.CompilerParams(
            dimension_semantics=("arbitrary",),
            vmem_limit_bytes=(8 << 20) + 4 * rows * slots + 6 * slots * width,
        ),
    )(
        jnp.reshape(core, (1,)).astype(jnp.int32),
        near,
        away,
        deg,
        feats,
        remote,
        w_self,
        w_neigh,
        pltpu.with_memory_space_constraint(cotangent, pltpu.HBM),
    )

    g = pltpu.with_memory_space_constraint(g, pltpu.HBM)
    dmsg = pltpu.with_memory_space_constraint(dmsg, pltpu.HBM)
    half = devices // 2
    twin = [(i, i ^ 1) for i in range(dom)]
    groups = [
        [d * sub + i for d in range(c, dom, 2) for i in range(sub)] for c in range(2)
    ]

    def exchange(x):
        return lax.all_to_all(
            x, AXES, split_axis=0, concat_axis=0, axis_index_groups=groups, tiled=True
        )

    far_cols = max(c for c in range(T, 4 * T, T) if far // 2 % c == 0)
    far_steps = far // 2 // far_cols

    def far_part(side, dmsg):
        return call(
            far_kernel,
            (far_steps,),
            [
                pl.BlockSpec((vcount, far_cols), lambda j: (0, j + side * far_steps)),
                pl.BlockSpec((vcount, width), whole),
            ],
            pl.BlockSpec((far_cols, width), by_row),
            jax.ShapeDtypeStruct((far // 2, width), bf16),
            "far",
            24 << 20,
        )(away, dmsg)

    sent = lax.dynamic_slice_in_dim(parts, (1 - core) * width, width, 0)
    kept = lax.dynamic_slice_in_dim(parts, core * width, width, 0)
    came = lax.ppermute(sent, "dom", twin)
    given = far_part(1, dmsg)
    got = lax.ppermute(given, "dom", twin)
    dmsg, given = tie(dmsg, given)
    kept_slots = far_part(0, dmsg)
    came, kept_slots = tie(came, kept_slots)
    share = width // half
    piece = (kept + came).astype(bf16).reshape(half, share, width)
    kept_slots = kept_slots.reshape(half, pack, width)
    got = got.reshape(half, pack, width)
    hub_sum = kept_slots[:, :hub_dev].astype(f32) + got[:, :hub_dev].astype(f32)
    payload = jnp.concatenate(
        [hub_sum.astype(bf16), kept_slots[:, hub_dev:], got[:, hub_dev:], piece], axis=1
    )
    bundle = payload.shape[1]
    returned = exchange(payload)
    cols = 2 * T
    base = call(
        own_kernel,
        (vcount // cols,),
        [
            pl.BlockSpec((vcount, cols), lambda j: (0, j)),
            pl.BlockSpec((vcount, width), whole),
            pl.BlockSpec((cols, width), by_row),
            pl.BlockSpec((width, width), whole),
        ],
        pl.BlockSpec((cols, width), by_row),
        jax.ShapeDtypeStruct((vcount, width), f32),
        "own",
        16 << 20,
    )(near, dmsg, g, w_self)

    mine = jnp.sum(returned[:, bundle - share :].astype(f32), axis=0).astype(bf16)
    mine, base = tie(mine, base)
    mine = exchange(jnp.broadcast_to(mine[None], (half, share, width))).reshape(width, width)
    table = send_rows.reshape(dom // 2, 2, sub, cap)
    same = lax.dynamic_index_in_dim(table, core, 1, keepdims=False).reshape(half, cap)
    cross = lax.dynamic_index_in_dim(table, 1 - core, 1, keepdims=False).reshape(half, cap)
    index = jnp.concatenate(
        [
            jnp.broadcast_to(hub_rows[None], (half, hub_dev)),
            same,
            cross,
            jnp.full((half, share), -1, jnp.int32),
        ],
        axis=1,
    ).reshape(1, half * bundle)
    grad_feats = call(
        finish_kernel,
        (vcount // rows,),
        [
            pl.BlockSpec((1, half * bundle), whole),
            pl.BlockSpec((rows, width), by_row),
            pl.BlockSpec((half * bundle, width), whole),
        ],
        pl.BlockSpec((rows, width), by_row),
        jax.ShapeDtypeStruct((vcount, width), bf16),
        "finish",
        (8 << 20) + 8 * far * width,
    )(index, base, returned.reshape(half * bundle, width))
    mine, grad_feats = tie(mine, grad_feats)
    other = lax.ppermute(mine, "dom", twin)
    grad_self = jnp.where(core == 0, mine, other).astype(f32)
    grad_neigh = jnp.where(core == 0, other, mine).astype(f32)
    return (layer_out, grad_feats, grad_self, grad_neigh)


def solution(mesh):
    return jax.shard_map(
        body,
        mesh=mesh,
        in_specs=(
            P(AXES, None),
            P(),
            P(),
            P(AXES, None),
            P(AXES),
            P(AXES),
            P(AXES),
            P(AXES),
        ),
        out_specs=(P(AXES, None), P(AXES, None), P(), P()),
        check_vma=False,
    )
```
